256 devices in a mesh: col: 32 (over x, y, core), sub: 8 (over z).
Axes of the slice: x: 4, y: 4, z: 8, core: 2. Of those that a mesh axis runs over, the one named last changes fastest.
Arguments:
- vectors: bfloat16 [1048576, 128], P(('col', 'sub')), may hold values from -6 to 6
- near_blocks: bfloat16 [4096, 4, 256, 256], P(('col', 'sub')), may hold values from -0.1875 to 0.1875
- near_index: int32 [4096, 4], P(('col', 'sub')), may hold values from 0 to 4095, as said below
- leaf_basis: bfloat16 [4096, 32, 256], P(('col', 'sub')), may hold values from -0.375 to 0.375
- leaf_transfer: float32 [4096, 32, 32], P(('col', 'sub')), may hold values from -0.25 to 0.25
- leaf_coupling: float32 [4096, 8, 32, 32], P(('col', 'sub')), may hold values from -0.375 to 0.375
- leaf_far: int32 [4096, 8], P(('col', 'sub')), may hold values from 0 to 4095, as said below
- cluster_transfer: float32 [256, 32, 32], P(('col', 'sub')), may hold values from -0.375 to 0.375
- cluster_coupling: float32 [256, 4, 32, 32], P(('col', 'sub')), may hold values from -0.5 to 0.5
- cluster_partner: int32 [256, 4], P(('col', 'sub')), may hold values from 0 to 7
- top_coupling: float32 [32, 8, 32, 32], P('col'), may hold values from -0.375 to 0.375
- top_partner: int32 [32, 8], P('col'), may hold values from 0 to 31
Outputs:
- products: bfloat16 [1048576, 128], P(('col', 'sub'))
The draws below stay inside these ranges and needn't reach their ends.
Inputs may be any that keep to these rules, and one draw needn't show every extreme that they name: `near_index`: slot 0 of leaf i is i itself; every entry lies within 16 leaves of i; slot 1 is exactly 16 leaves away from i. `leaf_far`: every entry lies within 16 leaves of its row leaf i; slots 0 and 1 are exactly 16 leaves away from i.
All inputs are finite; a program needn't handle non-finite values.
Results may differ from the reference program's by a relative error of at most 0.0034.
Values may be sent and summed in bfloat16 or wider, within the bound.
A program may use at most 64 MiB of HBM per device.

```python
import jax
import jax.numpy as jnp
from jax import lax

LEAF = 256
RANK = 32
LD = 16
NEAR = 4
FAR0 = 8
FAR1 = 4
FAR2 = 8
COLS = 128
LEAVES = 4096
NPTS = 1048576
N_COL = 32
N_SUB = 8


def draw_near_index(key, part):
    leaf_ids = jnp.arange(LEAVES, dtype=jnp.int32)
    stride = jnp.where(leaf_ids + LD < LEAVES, LD, -LD).astype(jnp.int32)
    offsets = jax.random.randint(jax.random.fold_in(key, 11), (LEAVES, NEAR - 2), -LD, LD + 1, dtype=jnp.int32)
    others = jnp.clip(leaf_ids[:, None] + offsets, 0, LEAVES - 1)
    return jnp.concatenate([leaf_ids[:, None], (leaf_ids + stride)[:, None], others], axis=1).astype(jnp.int32)


def draw_leaf_far(key, part):
    leaf_ids = jnp.arange(LEAVES, dtype=jnp.int32)
    first_slot = jnp.where(leaf_ids >= LD, leaf_ids - LD, leaf_ids + LD).astype(jnp.int32)
    second_slot = jnp.where(leaf_ids + LD < LEAVES, leaf_ids + LD, leaf_ids - LD).astype(jnp.int32)
    offsets = jax.random.randint(jax.random.fold_in(key, 23), (LEAVES, FAR0 - 2), -LD, LD + 1, dtype=jnp.int32)
    others = jnp.clip(leaf_ids[:, None] + offsets, 0, LEAVES - 1)
    return jnp.concatenate([first_slot[:, None], second_slot[:, None], others], axis=1).astype(jnp.int32)


def place_ends(array, key, least, high):
    longest = array.shape.index(max(array.shape))
    spots = []
    for shift in (0, 1):
        where = [jax.random.randint(jax.random.fold_in(key, axis), (), 0, length) for axis, length in enumerate(array.shape)]
        where[longest] = (where[longest] + shift) % array.shape[longest]
        spots.append(tuple(where))
    return array.at[spots[0]].set(least).at[spots[1]].set(high)


def levels(key, dims, split, low, largest):
    loudness, own = 1.0, jax.random.fold_in(key, 6)
    for axis_at, shards_of in split:
        heights = jnp.exp(jax.random.uniform(jax.random.fold_in(own, axis_at), (shards_of,), jnp.float32, low / len(split), largest / len(split)))
        loudness = loudness * jnp.repeat(heights, dims[axis_at] // shards_of).reshape([-1 if axis == axis_at else 1 for axis in range(len(dims))])
    return loudness


def scatter_about(key, dims, width, limit, cuts=(), kind=jnp.bfloat16):
    factor_of = levels(key, dims, cuts, -0.22, 0.18) if cuts else 1.0
    drawn = jax.random.normal(key, dims, jnp.float32) * width * factor_of
    return jnp.minimum(jnp.maximum(drawn, -limit), limit).astype(kind)


def setup_inputs(seed: int = 0) -> dict:
    splits = jax.random.split(jax.random.key(seed), 13)
    return {
        "vectors": scatter_about(splits[0], (NPTS, COLS), 1.0, 6.0, ((0, 256),)),
        "near_blocks": scatter_about(splits[1], (LEAVES, NEAR, LEAF, LEAF), (LEAF * NEAR) ** -0.5, 0.1875, ((0, 256),)),
        "near_index": draw_near_index(jax.random.fold_in(splits[12], 71), 0),
        "leaf_basis": scatter_about(splits[3], (LEAVES, RANK, LEAF), LEAF ** -0.5, 0.375, ((0, 256),)),
        "leaf_transfer": scatter_about(splits[4], (LEAVES, RANK, RANK), (RANK * LD) ** -0.5, 0.25, ((0, 256),), jnp.float32),
        "leaf_coupling": scatter_about(splits[5], (LEAVES, FAR0, RANK, RANK), (RANK * FAR0) ** -0.5, 0.375, ((0, 256),), jnp.float32),
        "leaf_far": draw_leaf_far(jax.random.fold_in(splits[12], 71), 0),
        "cluster_transfer": scatter_about(splits[7], (N_COL * N_SUB, RANK, RANK), (RANK * N_SUB) ** -0.5, 0.375, ((0, 256),), jnp.float32),
        "cluster_coupling": scatter_about(splits[8], (N_COL * N_SUB, FAR1, RANK, RANK), (RANK * FAR1) ** -0.5, 0.5, ((0, 256),), jnp.float32),
        "cluster_partner": place_ends(jax.random.randint(splits[9], (N_COL * N_SUB, FAR1), 0, N_SUB), jax.random.fold_in(splits[9], 1), 0, N_SUB - 1).astype(jnp.int32),
        "top_coupling": scatter_about(splits[10], (N_COL, FAR2, RANK, RANK), (RANK * FAR2) ** -0.5, 0.375, ((0, 32),), jnp.float32),
        "top_partner": place_ends(jax.random.randint(splits[11], (N_COL, FAR2), 0, N_COL), jax.random.fold_in(splits[11], 1), 0, N_COL - 1).astype(jnp.int32),
    }


HIGHEST = lax.Precision.HIGHEST


def reference(vectors, near_blocks, near_index, leaf_basis, leaf_transfer, leaf_coupling, leaf_far, cluster_transfer, cluster_coupling, cluster_partner, top_coupling, top_partner):
    group_count = N_COL * N_SUB
    leaf_count = group_count * LD
    leaf_vec = vectors.reshape(leaf_count, LEAF, COLS)

    def basis_apply(pieces):
        basis, local_vec = pieces
        return jnp.einsum('lrp,lpc->lrc', basis.astype(jnp.float32), local_vec.astype(jnp.float32), precision=HIGHEST)

    leaf_coefs = lax.map(basis_apply, (leaf_basis.reshape(group_count, LD, RANK, LEAF), leaf_vec.reshape(group_count, LD, LEAF, COLS))).reshape(leaf_count, RANK, COLS)
    cluster_coefs = jnp.einsum('lrs,lrc->lsc', leaf_transfer, leaf_coefs, precision=HIGHEST).reshape(group_count, LD, RANK, COLS).sum(axis=1)
    upward = jnp.einsum('drs,drc->dsc', cluster_transfer, cluster_coefs, precision=HIGHEST)
    top_coefs = upward.reshape(N_COL, N_SUB, RANK, COLS).sum(axis=1)
    top_field = jnp.einsum('qkrs,qksc->qrc', top_coupling, top_coefs[top_partner], precision=HIGHEST)
    group_base = (jnp.arange(group_count, dtype=jnp.int32) // N_SUB) * N_SUB
    partner_global = (group_base[:, None] + cluster_partner).astype(jnp.int32)
    cluster_field = jnp.einsum('dkrs,dksc->drc', cluster_coupling, cluster_coefs[partner_global], precision=HIGHEST)
    cluster_field = cluster_field + jnp.einsum('drs,dsc->drc', cluster_transfer, jnp.repeat(top_field, N_SUB, axis=0), precision=HIGHEST)

    def group_output(pieces):
        blocks, near_here, far_here, coupling, transfer, basis, parent = pieces
        leaf_field = jnp.einsum('lkrs,lksc->lrc', coupling, leaf_coefs[far_here], precision=HIGHEST)
        leaf_field = leaf_field + jnp.einsum('lrs,sc->lrc', transfer, parent, precision=HIGHEST)
        rounded = lax.optimization_barrier(leaf_field.astype(jnp.bfloat16)).astype(jnp.float32)
        picked = leaf_vec[near_here].astype(jnp.float32)
        near_part = jnp.einsum('lkij,lkjc->lic', blocks.astype(jnp.float32), picked, precision=HIGHEST)
        far_part = jnp.einsum('lrp,lrc->lpc', basis.astype(jnp.float32), rounded, precision=HIGHEST)
        return (near_part + far_part).astype(jnp.bfloat16)

    result = lax.map(group_output, (
        near_blocks.reshape(group_count, LD, NEAR, LEAF, LEAF),
        near_index.reshape(group_count, LD, NEAR),
        leaf_far.reshape(group_count, LD, FAR0),
        leaf_coupling.reshape(group_count, LD, FAR0, RANK, RANK),
        leaf_transfer.reshape(group_count, LD, RANK, RANK),
        leaf_basis.reshape(group_count, LD, RANK, LEAF),
        cluster_field))
    return result.reshape(leaf_count * LEAF, COLS)
```

```python
import functools

import jax
import jax.numpy as jnp
from jax import lax
from jax.experimental import pallas as pl
from jax.experimental.pallas import tpu as pltpu
from jax.sharding import PartitionSpec as P

MESH = pl.DeviceIdType.MESH
BF = jnp.bfloat16
F32 = jnp.float32


def matmul(a, b):
    return jnp.dot(a, b, preferred_element_type=F32)


def matmul_t(a, b):
    return lax.dot_general(a, b, (((0,), (0,)), ((), ())), preferred_element_type=F32)


def kernel(
    n_col,
    n_sub,
    first,
    vec,
    near_blocks,
    near_index,
    leaf_basis,
    leaf_transfer,
    leaf_coupling,
    leaf_far,
    cluster_transfer,
    cluster_coupling,
    cluster_partner,
    top_coupling,
    top_partner,
    out,
    own,
    win_a,
    win_b,
    blocks,
    basis,
    transfer,
    coupling,
    c_transfer,
    c_coupling,
    t_coupling,
    coefs,
    cwin,
    zsend,
    zbuf,
    tsend,
    tbuf,
    acc,
    local_sem,
    block_sem,
    bulk_send,
    bulk_recv,
    coef_send,
    coef_recv,
    z_send,
    z_recv,
    t_send,
    t_recv,
):
    leaves, rows, cols = own.shape
    near = blocks.shape[1]
    far0 = coupling.shape[1]
    rank = basis.shape[1]
    half = rows // 2
    col = lax.axis_index("col")
    sub = lax.axis_index("sub")
    here = col * n_sub + sub
    total = n_col * n_sub
    window_start = (here - 1) * leaves

    def device(index):
        return (index // n_sub, lax.rem(index, n_sub))

    def within(leaf):
        return jnp.minimum(jnp.maximum(leaf - window_start, 0), 3 * leaves - 1)

    following = device(lax.rem(here + 1, total))
    previous = device(lax.rem(here + total - 1, total))

    loads = [
        pltpu.make_async_copy(vec, own, local_sem.at[0]),
        pltpu.make_async_copy(leaf_basis, basis, local_sem.at[1]),
        pltpu.make_async_copy(leaf_transfer, transfer, local_sem.at[2]),
        pltpu.make_async_copy(cluster_transfer, c_transfer, local_sem.at[3]),
        pltpu.make_async_copy(cluster_coupling, c_coupling, local_sem.at[4]),
        pltpu.make_async_copy(top_coupling, t_coupling, local_sem.at[5]),
        pltpu.make_async_copy(vec.at[:, pl.ds(0, half)], win_a.at[pl.ds(leaves, leaves)], local_sem.at[6]),
        pltpu.make_async_copy(vec.at[:, pl.ds(half, half)], win_b.at[pl.ds(leaves, leaves)], local_sem.at[7]),
        pltpu.make_async_copy(leaf_coupling, coupling, local_sem.at[8]),
    ]
    for load in loads:
        load.start()
    block_load = pltpu.make_async_copy(near_blocks, blocks, block_sem)
    block_load.start()

    barrier = pltpu.get_barrier_semaphore()
    for target in (following, previous):
        pl.semaphore_signal(barrier, inc=1, device_id=target, device_id_type=MESH)

    def greet_sub(j, carry):
        pl.semaphore_signal(barrier, inc=1, device_id=(col, lax.rem(sub + j, n_sub)), device_id_type=MESH)
        return carry

    def greet_col(j, carry):
        pl.semaphore_signal(barrier, inc=1, device_id=(lax.rem(col + j, n_col), sub), device_id_type=MESH)
        return carry

    lax.fori_loop(1, n_sub, greet_sub, 0)
    lax.fori_loop(1, n_col, greet_col, 0)
    pl.semaphore_wait(barrier, 2 + (n_sub - 1) + (n_col - 1))

    def bulk(number, window, row, start, count):
        source = vec.at[pl.ds(start, count), pl.ds(row, half)]
        return [
            pltpu.make_async_remote_copy(
                src_ref=source,
                dst_ref=window.at[pl.ds(start, count)],
                send_sem=bulk_send.at[2 * number],
                recv_sem=bulk_recv.at[2 * number],
                device_id=following,
                device_id_type=MESH,
            ),
            pltpu.make_async_remote_copy(
                src_ref=source,
                dst_ref=window.at[pl.ds(2 * leaves + start, count)],
                send_sem=bulk_send.at[2 * number + 1],
                recv_sem=bulk_recv.at[2 * number + 1],
                device_id=previous,
                device_id_type=MESH,
            ),
        ]

    part_a = bulk(0, win_a, 0, 0, first) + bulk(1, win_a, 0, first, leaves - first)
    part_b = bulk(2, win_b, half, 0, leaves)
    for copy in part_a[:2]:
        copy.start()

    for load in loads[:3]:
        load.wait()

    for leaf in range(leaves):
        value = matmul(basis[leaf], own[leaf])
        coefs[leaf] = value.astype(BF)
        cwin[leaves + leaf] = value.astype(BF)
    for load in loads[3:6]:
        load.wait()
    cluster_coef = matmul_t(
        transfer[...].reshape(leaves * rank, rank).astype(BF), coefs[...].reshape(leaves * rank, cols)
    ).astype(BF)
    upward = matmul_t(c_transfer[0].astype(BF), cluster_coef)
    zsend[0] = cluster_coef
    zsend[1] = upward.astype(BF)
    z_copies = [
        pltpu.make_async_remote_copy(
            src_ref=zsend,
            dst_ref=zbuf.at[sub],
            send_sem=z_send.at[j],
            recv_sem=z_recv.at[j],
            device_id=(col, lax.rem(sub + j, n_sub)),
            device_id_type=MESH,
        )
        for j in range(1, n_sub)
    ]
    for copy in z_copies:
        copy.start()
    coef_copies = [
        pltpu.make_async_remote_copy(
            src_ref=coefs,
            dst_ref=cwin.at[pl.ds(2 * leaves * side, leaves)],
            send_sem=coef_send.at[side],
            recv_sem=coef_recv.at[side],
            device_id=target,
            device_id_type=MESH,
        )
        for side, target in enumerate((following, previous))
    ]
    for copy in coef_copies:
        copy.start()
    for copy in part_a[2:] + part_b:
        copy.start()

    keep_z = pltpu.make_async_copy(zsend, zbuf.at[sub], local_sem.at[9])
    keep_z.start()
    keep_z.wait()
    for copy in z_copies:
        copy.wait()

    top = zbuf[0, 1].astype(F32)
    for s in range(1, n_sub):
        top = top + zbuf[s, 1].astype(F32)
    tsend[...] = top.astype(BF)

    def top_copy(j):
        return pltpu.make_async_remote_copy(
            src_ref=tsend,
            dst_ref=tbuf.at[col],
            send_sem=t_send.at[j],
            recv_sem=t_recv.at[j],
            device_id=(lax.rem(col + j, n_col), sub),
            device_id_type=MESH,
        )

    def start_top(j, carry):
        top_copy(j).start()
        return carry

    def wait_top(j, carry):
        top_copy(j).wait()
        return carry

    lax.fori_loop(1, n_col, start_top, 0)
    keep_t = pltpu.make_async_copy(tsend, tbuf.at[col], local_sem.at[9])
    keep_t.start()

    cluster_field = jnp.zeros((rank, cols), F32)
    for k in range(c_coupling.shape[1]):
        cluster_field = cluster_field + matmul(c_coupling[0, k].astype(BF), zbuf[cluster_partner[0, k], 0])

    block_load.wait()

    def own_product(leaf, carry):
        acc[leaf] = matmul(blocks[leaf, 0], own[leaf])
        return carry

    lax.fori_loop(0, leaves, own_product, 0)

    keep_t.wait()
    lax.fori_loop(1, n_col, wait_top, 0)
    top_field = jnp.zeros((rank, cols), F32)
    for k in range(t_coupling.shape[1]):
        top_field = top_field + matmul(t_coupling[0, k].astype(BF), tbuf[top_partner[0, k]])
    cluster_field = cluster_field + matmul(c_transfer[0].astype(BF), top_field.astype(BF))
    parent = cluster_field.astype(BF)

    for load in loads[6:]:
        load.wait()
    for copy in coef_copies:
        copy.wait()

    def far_product(leaf, carry):
        field = matmul(transfer[leaf].astype(BF), parent)
        for k in range(far0):
            field = field + matmul(coupling[leaf, k].astype(BF), cwin[within(leaf_far[k, leaf])])
        acc[leaf] += matmul_t(basis[leaf], field.astype(BF))
        return carry

    lax.fori_loop(0, leaves, far_product, 0)

    def near_sum(leaf, window, start):
        index = [within(near_index[k, leaf]) for k in range(1, near)]
        left = jnp.concatenate([blocks[leaf, k, :, start : start + half] for k in range(1, near)], axis=1)
        right = jnp.concatenate([window[i] for i in index], axis=0)
        return acc[leaf] + matmul(left, right)

    for copy in part_a:
        copy.wait()

    def near_first(leaf, carry):
        acc[leaf] = near_sum(leaf, win_a, 0)
        return carry

    lax.fori_loop(0, leaves, near_first, 0)
    for copy in part_b:
        copy.wait()

    def near_second(leaf, carry):
        out[leaf] = near_sum(leaf, win_b, half).astype(BF)
        return carry

    lax.fori_loop(0, leaves, near_second, 0)


def local(n_col, n_sub, *args):
    (
        vectors,
        near_blocks,
        near_index,
        leaf_basis,
        leaf_transfer,
        leaf_coupling,
        leaf_far,
        cluster_transfer,
        cluster_coupling,
        cluster_partner,
        top_coupling,
        top_partner,
    ) = args
    leaves, rank, rows = leaf_basis.shape
    cols = vectors.shape[1]
    half = rows // 2
    anywhere = pl.BlockSpec(memory_space=pl.ANY)
    scalars = pl.BlockSpec(memory_space=pltpu.SMEM)
    dma = pltpu.SemaphoreType.DMA
    out = pl.pallas_call(
        functools.partial(kernel, n_col, n_sub, 4),
        out_shape=jax.ShapeDtypeStruct((leaves, rows, cols), BF),
        in_specs=[
            anywhere,
            anywhere,
            scalars,
            anywhere,
            anywhere,
            anywhere,
            scalars,
            anywhere,
            anywhere,
            scalars,
            anywhere,
            scalars,
        ],
        out_specs=pl.BlockSpec(memory_space=pltpu.VMEM),
        scratch_shapes=[
            pltpu.VMEM((leaves, rows, cols), BF),
            pltpu.VMEM((3 * leaves, half, cols), BF),
            pltpu.VMEM((3 * leaves, half, cols), BF),
            pltpu.VMEM(near_blocks.shape, BF),
            pltpu.VMEM(leaf_basis.shape, BF),
            pltpu.VMEM(leaf_transfer.shape, F32),
            pltpu.VMEM(leaf_coupling.shape, F32),
            pltpu.VMEM(cluster_transfer.shape, F32),
            pltpu.VMEM(cluster_coupling.shape, F32),
            pltpu.VMEM(top_coupling.shape, F32),
            pltpu.VMEM((leaves, rank, cols), BF),
            pltpu.VMEM((3 * leaves, rank, cols), BF),
            pltpu.VMEM((2, rank, cols), BF),
            pltpu.VMEM((n_sub, 2, rank, cols), BF),
            pltpu.VMEM((rank, cols), BF),
            pltpu.VMEM((n_col, rank, cols), BF),
            pltpu.VMEM((leaves, rows, cols), F32),
            dma((10,)),
            dma,
            dma((6,)),
            dma((6,)),
            dma((2,)),
            dma((2,)),
            dma((n_sub,)),
            dma((n_sub,)),
            dma((n_col,)),
            dma((n_col,)),
        ],
        compiler_params=pltpu.CompilerParams(collective_id=0, has_side_effects=True),
    )(
        vectors.reshape(leaves, rows, cols),
        near_blocks,
        near_index.T,
        leaf_basis,
        leaf_transfer,
        leaf_coupling,
        leaf_far.T,
        cluster_transfer,
        cluster_coupling,
        cluster_partner,
        top_coupling,
        top_partner,
    )
    return out.reshape(leaves * rows, cols)


def solution(mesh):
    leaf = ("col", "sub")
    in_specs = (
        P(leaf, None),
        P(leaf, None, None, None),
        P(leaf, None),
        P(leaf, None, None),
        P(leaf, None, None),
        P(leaf, None, None, None),
        P(leaf, None),
        P(leaf, None, None),
        P(leaf, None, None, None),
        P(leaf, None),
        P("col", None, None, None),
        P("col", None),
    )
    body = functools.partial(local, mesh.shape["col"], mesh.shape["sub"])
    return jax.shard_map(body, mesh=mesh, in_specs=in_specs, out_specs=P(leaf, None), check_vma=False)
```

```python
import functools

import jax
import jax.numpy as jnp
from jax import lax
from jax.experimental import pallas as pl
from jax.experimental.pallas import tpu as pltpu
from jax.sharding import PartitionSpec as P

MESH = pl.DeviceIdType.MESH
BF = jnp.bfloat16
F32 = jnp.float32


def matmul(a, b):
    return jnp.dot(a, b, preferred_element_type=F32)


def matmul_t(a, b):
    return lax.dot_general(a, b, (((0,), (0,)), ((), ())), preferred_element_type=F32)


def kernel(
    n_col,
    n_sub,
    first,
    vec,
    near_blocks,
    near_index,
    leaf_basis,
    leaf_transfer,
    leaf_coupling,
    leaf_far,
    cluster_transfer,
    cluster_coupling,
    cluster_partner,
    top_coupling,
    top_partner,
    out,
    own,
    win_a,
    win_b,
    blocks,
    packed,
    basis,
    transfer,
    coupling,
    c_transfer,
    c_coupling,
    t_coupling,
    coefs,
    cwin,
    zsend,
    zbuf,
    tsend,
    tbuf,
    field,
    acc,
    load_sem,
    bulk_send,
    bulk_recv,
    coef_send,
    coef_recv,
    z_send,
    z_recv,
    t_send,
    t_recv,
    known,
):
    leaves, rows, cols = own.shape
    near = blocks.shape[1]
    far0 = coupling.shape[1]
    rank = basis.shape[1]
    rows_a, rows_b = win_a.shape[1], win_b.shape[1]
    col = lax.axis_index("col")
    sub = lax.axis_index("sub")
    here = col * n_sub + sub
    total = n_col * n_sub
    window_start = (here - 1) * leaves
    has_next = here < total - 1
    has_prev = here > 0

    def within(leaf):
        return jnp.minimum(jnp.maximum(leaf - window_start, 0), 3 * leaves - 1)

    def device(index):
        return (index // n_sub, lax.rem(index, n_sub))

    following = device(lax.rem(here + 1, total))
    previous = device(lax.rem(here + total - 1, total))

    def at_col(step):
        return (lax.rem(col + step + n_col, n_col), sub)

    def at_sub(step):
        return (col, lax.rem(sub + step + n_sub, n_sub))

    def signal(sem, target):
        pl.semaphore_signal(sem, inc=1, device_id=target, device_id_type=MESH)

    barrier = pltpu.get_barrier_semaphore()
    signal(barrier, at_col(-1))

    @pl.when(has_prev)
    def _():
        signal(barrier, previous)

    @pl.when(sub == 0)
    def _():
        signal(barrier, at_sub(-1))

    own_load = pltpu.make_async_copy(vec, own, load_sem.at[0])
    basis_load = pltpu.make_async_copy(leaf_basis, basis, load_sem.at[1])
    transfer_loads = [
        pltpu.make_async_copy(leaf_transfer, transfer, load_sem.at[2]),
        pltpu.make_async_copy(cluster_transfer, c_transfer, load_sem.at[3]),
    ]
    block_load = pltpu.make_async_copy(near_blocks, blocks, load_sem.at[4])
    coupling_load = pltpu.make_async_copy(leaf_coupling, coupling, load_sem.at[5])
    window_loads = [
        pltpu.make_async_copy(vec.at[:, pl.ds(0, rows_a)], win_a.at[pl.ds(leaves, leaves)], load_sem.at[6]),
        pltpu.make_async_copy(vec.at[:, pl.ds(rows_a, rows_b)], win_b.at[pl.ds(leaves, leaves)], load_sem.at[7]),
    ]
    tree_loads = [
        pltpu.make_async_copy(cluster_coupling, c_coupling, load_sem.at[8]),
        pltpu.make_async_copy(top_coupling, t_coupling, load_sem.at[9]),
    ]
    for load in [own_load, basis_load] + transfer_loads:
        load.start()

    greeted = 1 + jnp.where(has_next, 1, 0) + jnp.where(sub == n_sub - 1, 1, 0)
    pl.semaphore_wait(barrier, greeted)

    def onward(number, source, window, send_sem, recv_sem):
        return pltpu.make_async_remote_copy(
            src_ref=source,
            dst_ref=window,
            send_sem=send_sem.at[number],
            recv_sem=recv_sem.at[number],
            device_id=following,
            device_id_type=MESH,
        )

    def backward(number, source, window, send_sem, recv_sem):
        return pltpu.make_async_remote_copy(
            src_ref=source,
            dst_ref=window,
            send_sem=send_sem.at[number],
            recv_sem=recv_sem.at[number],
            device_id=previous,
            device_id_type=MESH,
        )

    parts = [(win_a, 0, rows_a, 0, first), (win_a, 0, rows_a, first, leaves - first), (win_b, rows_a, rows_b, 0, leaves)]
    up, down = [], []
    for number, (window, row, height, start, count) in enumerate(parts):
        source = vec.at[pl.ds(start, count), pl.ds(row, height)]
        up.append(onward(2 * number, source, window.at[pl.ds(start, count)], bulk_send, bulk_recv))
        down.append(
            backward(2 * number + 1, source, window.at[pl.ds(2 * leaves + start, count)], bulk_send, bulk_recv)
        )
    coef_up = onward(0, coefs, cwin.at[pl.ds(0, leaves)], coef_send, coef_recv)
    coef_down = backward(1, coefs, cwin.at[pl.ds(2 * leaves, leaves)], coef_send, coef_recv)

    def start_up(copies):
        @pl.when(has_next)
        def _():
            for copy in copies:
                copy.start()

    def start_down(copies):
        @pl.when(has_prev)
        def _():
            for copy in copies:
                copy.start()

    def finish(up_copies, down_copies):
        @pl.when(has_next)
        def _():
            for copy in up_copies:
                copy.wait_send()
            for copy in down_copies:
                copy.wait_recv()

        @pl.when(has_prev)
        def _():
            for copy in up_copies:
                copy.wait_recv()
            for copy in down_copies:
                copy.wait_send()

    start_up(up[:1])

    signal(known.at[0], at_col(1))

    @pl.when(has_next)
    def _():
        signal(known.at[1], following)

    @pl.when(sub == n_sub - 1)
    def _():
        signal(known.at[2], at_sub(1))

    @pl.when(has_prev)
    def _():
        pl.semaphore_wait(known.at[1], 1)

    start_down(down[:1])

    @pl.when(sub == 0)
    def _():
        pl.semaphore_wait(known.at[2], 1)

    pl.semaphore_wait(known.at[0], 1)

    def tell(number, targets):
        for target in targets:
            signal(known.at[number], target)

    tell(3, (at_sub(1), at_sub(-1)))
    tell(4, (at_col(1), at_col(-1)))

    for load in window_loads + [block_load]:
        load.start()

    own_load.wait()
    basis_load.wait()
    for leaf in range(leaves):
        value = matmul(basis[leaf], own[leaf]).astype(BF)
        coefs[leaf] = value
        cwin[leaves + leaf] = value

    pl.semaphore_wait(known.at[3], 2)
    tell(5, (at_sub(2), at_sub(-2)))
    pl.semaphore_wait(known.at[4], 2)
    tell(6, (at_col(2), at_col(-2)))

    for load in transfer_loads:
        load.wait()
    cluster_coef = matmul_t(
        transfer[...].reshape(leaves * rank, rank).astype(BF), coefs[...].reshape(leaves * rank, cols)
    )
    zsend[0:rank] = cluster_coef.astype(BF)
    tall = rank * rank // cols
    zsend[rank : rank + tall] = jnp.concatenate(
        [c_transfer[0, tall * q : tall * (q + 1)] for q in range(rank // tall)], axis=1
    ).astype(BF)

    pl.semaphore_wait(known.at[5], 2)
    z_copies = [
        pltpu.make_async_remote_copy(
            src_ref=zsend,
            dst_ref=zbuf.at[sub],
            send_sem=z_send.at[j],
            recv_sem=z_recv.at[j],
            device_id=at_sub(j),
            device_id_type=MESH,
        )
        for j in range(1, n_sub)
    ]
    for copy in z_copies:
        copy.start()
    start_up([coef_up] + up[1:])
    start_down([coef_down] + down[1:])
    keep_z = pltpu.make_async_copy(zsend, zbuf.at[sub], load_sem.at[10])
    keep_z.start()
    for load in [coupling_load] + tree_loads:
        load.start()
    pl.semaphore_wait(known.at[6], 2)
    tell(7, (at_col(4), at_col(-4)))

    block_load.wait()

    def own_product(leaf, carry):
        acc[leaf] = matmul(blocks[leaf, 0], own[leaf])
        packed[leaf] = jnp.concatenate([blocks[leaf, k, :, rows_a:rows] for k in range(1, near)], axis=1)
        return carry

    lax.fori_loop(0, leaves // 2, own_product, 0)
    pl.semaphore_wait(known.at[7], 2)
    tell(8, (at_col(8), at_col(-8)))
    lax.fori_loop(leaves // 2, leaves, own_product, 0)

    keep_z.wait()
    for copy in z_copies:
        copy.wait()
    gathered = zbuf[...].astype(F32)
    top = jnp.zeros((rank, cols), F32)
    for q in range(rank // tall):
        left = gathered[:, rank : rank + tall, rank * q : rank * (q + 1)].reshape(n_sub * tall, rank)
        right = gathered[:, tall * q : tall * (q + 1)].reshape(n_sub * tall, cols)
        top = top + matmul_t(left.astype(BF), right.astype(BF))
    tsend[...] = top.astype(BF)

    def top_copy(j):
        return pltpu.make_async_remote_copy(
            src_ref=tsend,
            dst_ref=tbuf.at[col],
            send_sem=t_send.at[j],
            recv_sem=t_recv.at[j],
            device_id=at_col(j),
            device_id_type=MESH,
        )

    def start_top(j, carry):
        top_copy(j).start()
        return carry

    def wait_top(j, carry):
        top_copy(j).wait()
        return carry

    pl.semaphore_wait(known.at[8], 2)
    lax.fori_loop(1, n_col, start_top, 0)
    keep_t = pltpu.make_async_copy(tsend, tbuf.at[col], load_sem.at[10])
    keep_t.start()

    for load in [coupling_load] + tree_loads:
        load.wait()
    cluster_field = jnp.zeros((rank, cols), F32)
    for k in range(c_coupling.shape[1]):
        cluster_field = cluster_field + matmul(c_coupling[0, k].astype(BF), zbuf[cluster_partner[0, k], 0:rank])

    finish([coef_up], [coef_down])

    def far_sum(leaf, carry):
        left = jnp.concatenate([coupling[leaf, k] for k in range(far0)], axis=1).astype(BF)
        right = jnp.concatenate([cwin[within(leaf_far[k, leaf])] for k in range(far0)], axis=0)
        field[leaf] = matmul(left, right)
        return carry

    lax.fori_loop(0, leaves, far_sum, 0)

    keep_t.wait()
    lax.fori_loop(1, n_col, wait_top, 0)
    top_field = jnp.zeros((rank, cols), F32)
    for k in range(t_coupling.shape[1]):
        top_field = top_field + matmul(t_coupling[0, k].astype(BF), tbuf[top_partner[0, k]])
    cluster_field = cluster_field + matmul(c_transfer[0].astype(BF), top_field.astype(BF))
    parent = cluster_field.astype(BF)

    def far_product(leaf, carry):
        value = field[leaf] + matmul(transfer[leaf].astype(BF), parent)
        acc[leaf] += matmul_t(basis[leaf], value.astype(BF))
        return carry

    lax.fori_loop(0, leaves, far_product, 0)

    for load in window_loads:
        load.wait()
    finish(up[:2], down[:2])

    def near_first(leaf, carry):
        value = acc[leaf]
        for k in range(1, near):
            value = value + matmul(blocks[leaf, k, :, 0:rows_a], win_a[within(near_index[k, leaf])])
        acc[leaf] = value
        return carry

    lax.fori_loop(0, leaves, near_first, 0)
    finish(up[2:], down[2:])

    def near_second(leaf, carry):
        right = jnp.concatenate([win_b[within(near_index[k, leaf])] for k in range(1, near)], axis=0)
        out[leaf] = (acc[leaf] + matmul(packed[leaf], right)).astype(BF)
        return carry

    lax.fori_loop(0, leaves, near_second, 0, unroll=True)


def local(n_col, n_sub, *args):
    (
        vectors,
        near_blocks,
        near_index,
        leaf_basis,
        leaf_transfer,
        leaf_coupling,
        leaf_far,
        cluster_transfer,
        cluster_coupling,
        cluster_partner,
        top_coupling,
        top_partner,
    ) = args
    leaves, rank, rows = leaf_basis.shape
    near = near_blocks.shape[1]
    cols = vectors.shape[1]
    rows_b = rows // 4
    rows_a = rows - rows_b
    anywhere = pl.BlockSpec(memory_space=pl.ANY)
    scalars = pl.BlockSpec(memory_space=pltpu.SMEM)
    dma = pltpu.SemaphoreType.DMA
    out = pl.pallas_call(
        functools.partial(kernel, n_col, n_sub, 3),
        out_shape=pltpu.VMEM((leaves, rows, cols), BF),
        in_specs=[
            anywhere,
            anywhere,
            scalars,
            anywhere,
            anywhere,
            anywhere,
            scalars,
            anywhere,
            anywhere,
            scalars,
            anywhere,
            scalars,
        ],
        out_specs=pl.BlockSpec(memory_space=pltpu.VMEM),
        scratch_shapes=[
            pltpu.VMEM((leaves, rows, cols), BF),
            pltpu.VMEM((3 * leaves, rows_a, cols), BF),
            pltpu.VMEM((3 * leaves, rows_b, cols), BF),
            pltpu.VMEM(near_blocks.shape, BF),
            pltpu.VMEM((leaves, rows, (near - 1) * rows_b), BF),
            pltpu.VMEM(leaf_basis.shape, BF),
            pltpu.VMEM(leaf_transfer.shape, F32),
            pltpu.VMEM(leaf_coupling.shape, F32),
            pltpu.VMEM(cluster_transfer.shape, F32),
            pltpu.VMEM(cluster_coupling.shape, F32),
            pltpu.VMEM(top_coupling.shape, F32),
            pltpu.VMEM((leaves, rank, cols), BF),
            pltpu.VMEM((3 * leaves, rank, cols), BF),
            pltpu.VMEM((rank + rank * rank // cols, cols), BF),
            pltpu.VMEM((n_sub, rank + rank * rank // cols, cols), BF),
            pltpu.VMEM((rank, cols), BF),
            pltpu.VMEM((n_col, rank, cols), BF),
            pltpu.VMEM((leaves, rank, cols), F32),
            pltpu.VMEM((leaves, rows, cols), F32),
            dma((11,)),
            dma((6,)),
            dma((6,)),
            dma((2,)),
            dma((2,)),
            dma((n_sub,)),
            dma((n_sub,)),
            dma((n_col,)),
            dma((n_col,)),
            pltpu.SemaphoreType.REGULAR((9,)),
        ],
        compiler_params=pltpu.CompilerParams(collective_id=0, has_side_effects=True),
    )(
        vectors.reshape(leaves, rows, cols),
        near_blocks,
        near_index.T,
        leaf_basis,
        leaf_transfer,
        leaf_coupling,
        leaf_far.T,
        cluster_transfer,
        cluster_coupling,
        cluster_partner,
        top_coupling,
        top_partner,
    )
    return out.reshape(leaves * rows, cols)


def solution(mesh):
    leaf = ("col", "sub")
    in_specs = (
        P(leaf, None),
        P(leaf, None, None, None),
        P(leaf, None),
        P(leaf, None, None),
        P(leaf, None, None),
        P(leaf, None, None, None),
        P(leaf, None),
        P(leaf, None, None),
        P(leaf, None, None, None),
        P(leaf, None),
        P("col", None, None, None),
        P("col", None),
    )
    body = functools.partial(local, mesh.shape["col"], mesh.shape["sub"])
    return jax.shard_map(body, mesh=mesh, in_specs=in_specs, out_specs=P(leaf, None), check_vma=False)
```

```python
import functools
import math

import jax
import jax.numpy as jnp
from jax import lax
from jax.experimental import pallas as pl
from jax.experimental.pallas import tpu as pltpu
from jax.sharding import PartitionSpec as P

MESH = pl.DeviceIdType.MESH
BF = jnp.bfloat16
F32 = jnp.float32


def matmul(a, b):
    return jnp.dot(a, b, preferred_element_type=F32)


def matmul_t(a, b):
    return lax.dot_general(a, b, (((0,), (0,)), ((), ())), preferred_element_type=F32)


def kernel(
    n_col,
    n_sub,
    side,
    first,
    vec,
    near_blocks,
    near_table,
    leaf_basis,
    leaf_transfer,
    leaf_coupling,
    far_table,
    cluster_transfer,
    cluster_coupling,
    cluster_table,
    top_coupling,
    top_table,
    out,
    own,
    win_a,
    win_b,
    blocks,
    packed,
    basis,
    transfer,
    coupling,
    c_transfer,
    c_coupling,
    t_coupling,
    coefs,
    cwin,
    zsend,
    zbuf,
    tsend,
    tbuf,
    field,
    acc,
    load_sem,
    bulk_send,
    bulk_recv,
    coef_send,
    coef_recv,
    z_send,
    z_recv,
    t_send,
    t_recv,
    known,
    table_sem,
    near_index,
    leaf_far,
    cluster_partner,
    top_partner,
):
    leaves, rows, cols = own.shape
    near = blocks.shape[1]
    far0 = coupling.shape[1]
    rank = basis.shape[1]
    rows_a, rows_b = win_a.shape[1], win_b.shape[1]
    col = lax.axis_index("col")
    sub = lax.axis_index("sub")
    here = col * n_sub + sub
    total = n_col * n_sub
    window_start = (here - 1) * leaves
    has_next = here < total - 1
    has_prev = here > 0

    def within(leaf):
        return jnp.minimum(jnp.maximum(leaf - window_start, 0), 3 * leaves - 1)

    def device(index):
        return (index // n_sub, lax.rem(index, n_sub))

    following = device(lax.rem(here + 1, total))
    previous = device(lax.rem(here + total - 1, total))

    def at_col(step):
        return (lax.rem(col + step + n_col, n_col), sub)

    def walk(position):
        line, place = position // (2 * side), lax.rem(position, 2 * side)
        chip, core = place // 2, lax.rem(place, 2)
        odd = lax.rem(line, 2)
        return line * 2 * side + (odd * (side - 1) + (1 - 2 * odd) * chip) * 2 + core

    def along(step):
        return (walk(lax.rem(walk(col) + step + n_col, n_col)), sub)

    def at_sub(step):
        return (col, lax.rem(sub + step + n_sub, n_sub))

    def signal(sem, target):
        pl.semaphore_signal(sem, inc=1, device_id=target, device_id_type=MESH)

    barrier = pltpu.get_barrier_semaphore()
    signal(barrier, along(-1))

    @pl.when(has_prev)
    def _():
        signal(barrier, previous)

    @pl.when(sub == 0)
    def _():
        signal(barrier, at_sub(-1))

    own_load = pltpu.make_async_copy(vec, own, load_sem.at[0])
    basis_load = pltpu.make_async_copy(leaf_basis, basis, load_sem.at[1])
    transfer_loads = [
        pltpu.make_async_copy(leaf_transfer, transfer, load_sem.at[2]),
        pltpu.make_async_copy(cluster_transfer, c_transfer, load_sem.at[3]),
    ]
    block_load = pltpu.make_async_copy(near_blocks, blocks, load_sem.at[4])
    coupling_load = pltpu.make_async_copy(leaf_coupling, coupling, load_sem.at[5])
    window_loads = [
        pltpu.make_async_copy(vec.at[:, pl.ds(0, rows_a)], win_a.at[pl.ds(leaves, leaves)], load_sem.at[6]),
        pltpu.make_async_copy(vec.at[:, pl.ds(rows_a, rows_b)], win_b.at[pl.ds(leaves, leaves)], load_sem.at[7]),
    ]
    tree_loads = [
        pltpu.make_async_copy(cluster_coupling, c_coupling, load_sem.at[8]),
        pltpu.make_async_copy(top_coupling, t_coupling, load_sem.at[9]),
    ]
    for load in [own_load, basis_load] + transfer_loads:
        load.start()

    greeted = 1 + jnp.where(has_next, 1, 0) + jnp.where(sub == n_sub - 1, 1, 0)
    pl.semaphore_wait(barrier, greeted)

    def onward(number, source, window, send_sem, recv_sem):
        return pltpu.make_async_remote_copy(
            src_ref=source,
            dst_ref=window,
            send_sem=send_sem.at[number],
            recv_sem=recv_sem.at[number],
            device_id=following,
            device_id_type=MESH,
        )

    def backward(number, source, window, send_sem, recv_sem):
        return pltpu.make_async_remote_copy(
            src_ref=source,
            dst_ref=window,
            send_sem=send_sem.at[number],
            recv_sem=recv_sem.at[number],
            device_id=previous,
            device_id_type=MESH,
        )

    parts = [(win_a, 0, rows_a, 0, first), (win_a, 0, rows_a, first, leaves - first), (win_b, rows_a, rows_b, 0, leaves)]
    up, down = [], []
    for number, (window, row, height, start, count) in enumerate(parts):
        source = vec.at[pl.ds(start, count), pl.ds(row, height)]
        up.append(onward(2 * number, source, window.at[pl.ds(start, count)], bulk_send, bulk_recv))
        down.append(
            backward(2 * number + 1, source, window.at[pl.ds(2 * leaves + start, count)], bulk_send, bulk_recv)
        )
    coef_up = onward(0, coefs, cwin.at[pl.ds(0, leaves)], coef_send, coef_recv)
    coef_down = backward(1, coefs, cwin.at[pl.ds(2 * leaves, leaves)], coef_send, coef_recv)

    def start_up(copies):
        @pl.when(has_next)
        def _():
            for copy in copies:
                copy.start()

    def start_down(copies):
        @pl.when(has_prev)
        def _():
            for copy in copies:
                copy.start()

    def finish(up_copies, down_copies):
        @pl.when(has_next)
        def _():
            for copy in up_copies:
                copy.wait_send()
            for copy in down_copies:
                copy.wait_recv()

        @pl.when(has_prev)
        def _():
            for copy in up_copies:
                copy.wait_recv()
            for copy in down_copies:
                copy.wait_send()

    start_up(up[:1])

    signal(known.at[0], along(1))

    @pl.when(has_next)
    def _():
        signal(known.at[1], following)

    @pl.when(sub == n_sub - 1)
    def _():
        signal(known.at[2], at_sub(1))

    @pl.when(has_prev)
    def _():
        pl.semaphore_wait(known.at[1], 1)

    start_down(down[:1])

    @pl.when(sub == 0)
    def _():
        pl.semaphore_wait(known.at[2], 1)

    def tell(number, targets):
        for target in targets:
            signal(known.at[number], target)

    tell(3, (at_sub(1), at_sub(-1)))

    for load in window_loads + [block_load]:
        load.start()

    own_load.wait()
    basis_load.wait()
    for leaf in range(leaves):
        value = matmul(basis[leaf], own[leaf]).astype(BF)
        coefs[leaf] = value
        cwin[leaves + leaf] = value

    pl.semaphore_wait(known.at[3], 2)
    tell(5, (at_sub(2), at_sub(-2)))
    pl.semaphore_wait(known.at[0], 1)
    tell(4, (along(1), along(-1)))

    for load in transfer_loads:
        load.wait()
    cluster_coef = matmul_t(
        transfer[...].reshape(leaves * rank, rank).astype(BF), coefs[...].reshape(leaves * rank, cols)
    )
    zsend[0:rank] = cluster_coef.astype(BF)
    tall = rank * rank // cols
    zsend[rank : rank + tall] = jnp.concatenate(
        [c_transfer[0, tall * q : tall * (q + 1)] for q in range(rank // tall)], axis=1
    ).astype(BF)

    pl.semaphore_wait(known.at[5], 2)
    z_copies = [
        pltpu.make_async_remote_copy(
            src_ref=zsend,
            dst_ref=zbuf.at[sub],
            send_sem=z_send.at[j],
            recv_sem=z_recv.at[j],
            device_id=at_sub(j),
            device_id_type=MESH,
        )
        for j in range(1, n_sub)
    ]
    for copy in z_copies:
        copy.start()
    start_up([coef_up] + up[1:])
    start_down([coef_down] + down[1:])
    keep_z = pltpu.make_async_copy(zsend, zbuf.at[sub], load_sem.at[10])
    keep_z.start()
    table_loads = [
        pltpu.make_async_copy(source, target, table_sem.at[i])
        for i, (source, target) in enumerate(
            ((near_table, near_index), (far_table, leaf_far), (cluster_table, cluster_partner), (top_table, top_partner))
        )
    ]
    for load in [coupling_load] + tree_loads + table_loads:
        load.start()
    pl.semaphore_wait(known.at[4], 2)
    tell(6, (along(2), along(-2)))

    block_load.wait()

    def own_product(leaf, carry):
        acc[leaf] = matmul(blocks[leaf, 0], own[leaf])
        packed[leaf] = jnp.concatenate([blocks[leaf, k, :, rows_a:rows] for k in range(1, near)], axis=1)
        return carry

    lax.fori_loop(0, leaves // 2, own_product, 0)
    pl.semaphore_wait(known.at[6], 2)
    tell(7, (along(4), along(-4)))
    lax.fori_loop(leaves // 2, leaves, own_product, 0)
    pl.semaphore_wait(known.at[7], 2)
    tell(8, (along(8), along(-8)))

    keep_z.wait()
    for copy in z_copies:
        copy.wait()
    gathered = zbuf[...].astype(F32)
    top = jnp.zeros((rank, cols), F32)
    for q in range(rank // tall):
        left = gathered[:, rank : rank + tall, rank * q : rank * (q + 1)].reshape(n_sub * tall, rank)
        right = gathered[:, tall * q : tall * (q + 1)].reshape(n_sub * tall, cols)
        top = top + matmul_t(left.astype(BF), right.astype(BF))
    tsend[...] = top.astype(BF)

    def top_copy(j):
        return pltpu.make_async_remote_copy(
            src_ref=tsend,
            dst_ref=tbuf.at[col],
            send_sem=t_send.at[j],
            recv_sem=t_recv.at[j],
            device_id=at_col(j),
            device_id_type=MESH,
        )

    def start_top(j, carry):
        top_copy(j).start()
        return carry

    def wait_top(j, carry):
        top_copy(j).wait()
        return carry

    pl.semaphore_wait(known.at[8], 2)
    lax.fori_loop(1, n_col, start_top, 0)
    keep_t = pltpu.make_async_copy(tsend, tbuf.at[col], load_sem.at[10])
    keep_t.start()

    for load in [coupling_load] + tree_loads + table_loads:
        load.wait()
    cluster_field = jnp.zeros((rank, cols), F32)
    for k in range(c_coupling.shape[1]):
        cluster_field = cluster_field + matmul(c_coupling[0, k].astype(BF), zbuf[cluster_partner[0, k], 0:rank])

    finish([coef_up], [coef_down])

    def far_sum(leaf, carry):
        left = jnp.concatenate([coupling[leaf, k] for k in range(far0)], axis=1).astype(BF)
        right = jnp.concatenate([cwin[within(leaf_far[k, leaf])] for k in range(far0)], axis=0)
        field[leaf] = matmul(left, right)
        return carry

    lax.fori_loop(0, leaves, far_sum, 0)

    keep_t.wait()
    lax.fori_loop(1, n_col, wait_top, 0)
    top_field = jnp.zeros((rank, cols), F32)
    for k in range(t_coupling.shape[1]):
        top_field = top_field + matmul(t_coupling[0, k].astype(BF), tbuf[top_partner[0, k]])
    cluster_field = cluster_field + matmul(c_transfer[0].astype(BF), top_field.astype(BF))
    parent = cluster_field.astype(BF)

    def far_product(leaf, carry):
        value = field[leaf] + matmul(transfer[leaf].astype(BF), parent)
        acc[leaf] += matmul_t(basis[leaf], value.astype(BF))
        return carry

    lax.fori_loop(0, leaves, far_product, 0)

    for load in window_loads:
        load.wait()
    finish(up[:2], down[:2])

    def near_first(leaf, carry):
        value = acc[leaf]
        for k in range(1, near):
            value = value + matmul(blocks[leaf, k, :, 0:rows_a], win_a[within(near_index[k, leaf])])
        acc[leaf] = value
        return carry

    lax.fori_loop(0, leaves, near_first, 0)
    finish(up[2:], down[2:])

    def near_second(leaf, carry):
        right = jnp.concatenate([win_b[within(near_index[k, leaf])] for k in range(1, near)], axis=0)
        out[leaf] = (acc[leaf] + matmul(packed[leaf], right)).astype(BF)
        return carry

    lax.fori_loop(0, leaves, near_second, 0, unroll=True)


def local(n_col, n_sub, *args):
    (
        vectors,
        near_blocks,
        near_index,
        leaf_basis,
        leaf_transfer,
        leaf_coupling,
        leaf_far,
        cluster_transfer,
        cluster_coupling,
        cluster_partner,
        top_coupling,
        top_partner,
    ) = args
    leaves, rank, rows = leaf_basis.shape
    near = near_blocks.shape[1]
    cols = vectors.shape[1]
    rows_b = rows // 4
    rows_a = rows - rows_b
    anywhere = pl.BlockSpec(memory_space=pl.ANY)
    scalars = anywhere
    dma = pltpu.SemaphoreType.DMA
    out = pl.pallas_call(
        functools.partial(kernel, n_col, n_sub, math.isqrt(n_col // 2), 4),
        out_shape=pltpu.VMEM((leaves, rows, cols), BF),
        in_specs=[
            anywhere,
            anywhere,
            scalars,
            anywhere,
            anywhere,
            anywhere,
            scalars,
            anywhere,
            anywhere,
            scalars,
            anywhere,
            scalars,
        ],
        out_specs=pl.BlockSpec(memory_space=pltpu.VMEM),
        scratch_shapes=[
            pltpu.VMEM((leaves, rows, cols), BF),
            pltpu.VMEM((3 * leaves, rows_a, cols), BF),
            pltpu.VMEM((3 * leaves, rows_b, cols), BF),
            pltpu.VMEM(near_blocks.shape, BF),
            pltpu.VMEM((leaves, rows, (near - 1) * rows_b), BF),
            pltpu.VMEM(leaf_basis.shape, BF),
            pltpu.VMEM(leaf_transfer.shape, F32),
            pltpu.VMEM(leaf_coupling.shape, F32),
            pltpu.VMEM(cluster_transfer.shape, F32),
            pltpu.VMEM(cluster_coupling.shape, F32),
            pltpu.VMEM(top_coupling.shape, F32),
            pltpu.VMEM((leaves, rank, cols), BF),
            pltpu.VMEM((3 * leaves, rank, cols), BF),
            pltpu.VMEM((rank + rank * rank // cols, cols), BF),
            pltpu.VMEM((n_sub, rank + rank * rank // cols, cols), BF),
            pltpu.VMEM((rank, cols), BF),
            pltpu.VMEM((n_col, rank, cols), BF),
            pltpu.VMEM((leaves, rank, cols), F32),
            pltpu.VMEM((leaves, rows, cols), F32),
            dma((11,)),
            dma((6,)),
            dma((6,)),
            dma((2,)),
            dma((2,)),
            dma((n_sub,)),
            dma((n_sub,)),
            dma((n_col,)),
            dma((n_col,)),
            pltpu.SemaphoreType.REGULAR((9,)),
            dma((4,)),
            pltpu.SMEM((near, leaves), jnp.int32),
            pltpu.SMEM((leaf_far.shape[1], leaves), jnp.int32),
            pltpu.SMEM(cluster_partner.shape, jnp.int32),
            pltpu.SMEM(top_partner.shape, jnp.int32),
        ],
        compiler_params=pltpu.CompilerParams(collective_id=0, has_side_effects=True),
    )(
        vectors.reshape(leaves, rows, cols),
        near_blocks,
        near_index.T,
        leaf_basis,
        leaf_transfer,
        leaf_coupling,
        leaf_far.T,
        cluster_transfer,
        cluster_coupling,
        cluster_partner,
        top_coupling,
        top_partner,
    )
    return out.reshape(leaves * rows, cols)


def solution(mesh):
    leaf = ("col", "sub")
    in_specs = (
        P(leaf, None),
        P(leaf, None, None, None),
        P(leaf, None),
        P(leaf, None, None),
        P(leaf, None, None),
        P(leaf, None, None, None),
        P(leaf, None),
        P(leaf, None, None),
        P(leaf, None, None, None),
        P(leaf, None),
        P("col", None, None, None),
        P("col", None),
    )
    body = functools.partial(local, mesh.shape["col"], mesh.shape["sub"])
    return jax.shard_map(body, mesh=mesh, in_specs=in_specs, out_specs=P(leaf, None), check_vma=False)
```

```python
import functools
import math

import jax
import jax.numpy as jnp
from jax import lax
from jax.experimental import pallas as pl
from jax.experimental.pallas import tpu as pltpu
from jax.sharding import PartitionSpec as P

MESH = pl.DeviceIdType.MESH
BF = jnp.bfloat16
F32 = jnp.float32


def matmul(a, b):
    return jnp.dot(a, b, preferred_element_type=F32)


def matmul_t(a, b):
    return lax.dot_general(a, b, (((0,), (0,)), ((), ())), preferred_element_type=F32)


def kernel(
    n_col,
    n_sub,
    side,
    first,
    more,
    vec,
    near_blocks,
    near_table,
    leaf_basis,
    leaf_transfer,
    leaf_coupling,
    far_table,
    cluster_transfer,
    cluster_coupling,
    cluster_table,
    top_coupling,
    top_table,
    out,
    own,
    win_a,
    win_b,
    blocks,
    packed,
    basis,
    transfer,
    coupling,
    c_transfer,
    c_coupling,
    t_coupling,
    coefs,
    cwin,
    zsend,
    zbuf,
    tsend,
    tbuf,
    field,
    acc,
    load_sem,
    bulk_send,
    bulk_recv,
    coef_send,
    coef_recv,
    z_send,
    z_recv,
    t_send,
    t_recv,
    known,
    table_sem,
    near_index,
    leaf_far,
    cluster_partner,
    top_partner,
):
    leaves, rows, cols = own.shape
    near = blocks.shape[1]
    far0 = coupling.shape[1]
    rank = basis.shape[1]
    rows_a, rows_b = win_a.shape[1], win_b.shape[1]
    col = lax.axis_index("col")
    sub = lax.axis_index("sub")
    here = col * n_sub + sub
    total = n_col * n_sub
    window_start = (here - 1) * leaves
    has_next = here < total - 1
    has_prev = here > 0

    def within(leaf):
        return jnp.minimum(jnp.maximum(leaf - window_start, 0), 3 * leaves - 1)

    def device(index):
        return (index // n_sub, lax.rem(index, n_sub))

    following = device(lax.rem(here + 1, total))
    previous = device(lax.rem(here + total - 1, total))

    def at_col(step):
        return (lax.rem(col + step + n_col, n_col), sub)

    def walk(position):
        line, place = position // (2 * side), lax.rem(position, 2 * side)
        chip, core = place // 2, lax.rem(place, 2)
        odd = lax.rem(line, 2)
        return line * 2 * side + (odd * (side - 1) + (1 - 2 * odd) * chip) * 2 + core

    def along(step):
        return (walk(lax.rem(walk(col) + step + n_col, n_col)), sub)

    def at_sub(step):
        return (col, lax.rem(sub + step + n_sub, n_sub))

    def signal(sem, target):
        pl.semaphore_signal(sem, inc=1, device_id=target, device_id_type=MESH)

    barrier = pltpu.get_barrier_semaphore()
    signal(barrier, along(-1))

    @pl.when(has_prev)
    def _():
        signal(barrier, previous)

    @pl.when(sub == 0)
    def _():
        signal(barrier, at_sub(-1))

    own_load = pltpu.make_async_copy(vec, own, load_sem.at[0])
    basis_load = pltpu.make_async_copy(leaf_basis, basis, load_sem.at[1])
    transfer_loads = [
        pltpu.make_async_copy(leaf_transfer, transfer, load_sem.at[2]),
        pltpu.make_async_copy(cluster_transfer, c_transfer, load_sem.at[3]),
    ]
    block_load = pltpu.make_async_copy(near_blocks, blocks, load_sem.at[4])
    coupling_load = pltpu.make_async_copy(leaf_coupling, coupling, load_sem.at[5])
    window_loads = [
        pltpu.make_async_copy(vec.at[:, pl.ds(0, rows_a)], win_a.at[pl.ds(leaves, leaves)], load_sem.at[6]),
        pltpu.make_async_copy(vec.at[:, pl.ds(rows_a, rows_b)], win_b.at[pl.ds(leaves, leaves)], load_sem.at[7]),
    ]
    tree_loads = [
        pltpu.make_async_copy(cluster_coupling, c_coupling, load_sem.at[8]),
        pltpu.make_async_copy(top_coupling, t_coupling, load_sem.at[9]),
    ]
    for load in [own_load, basis_load] + transfer_loads:
        load.start()

    greeted = 1 + jnp.where(has_next, 1, 0) + jnp.where(sub == n_sub - 1, 1, 0)
    pl.semaphore_wait(barrier, greeted)

    def onward(number, source, window, send_sem, recv_sem):
        return pltpu.make_async_remote_copy(
            src_ref=source,
            dst_ref=window,
            send_sem=send_sem.at[number],
            recv_sem=recv_sem.at[number],
            device_id=following,
            device_id_type=MESH,
        )

    def backward(number, source, window, send_sem, recv_sem):
        return pltpu.make_async_remote_copy(
            src_ref=source,
            dst_ref=window,
            send_sem=send_sem.at[number],
            recv_sem=recv_sem.at[number],
            device_id=previous,
            device_id_type=MESH,
        )

    parts = [
        (win_a, 0, rows_a, 0, first),
        (win_a, 0, rows_a, first, more),
        (win_a, 0, rows_a, first + more, leaves - first - more),
        (win_b, rows_a, rows_b, 0, leaves),
    ]
    up, down = [], []
    for number, (window, row, height, start, count) in enumerate(parts):
        source = vec.at[pl.ds(start, count), pl.ds(row, height)]
        up.append(onward(2 * number, source, window.at[pl.ds(start, count)], bulk_send, bulk_recv))
        down.append(
            backward(2 * number + 1, source, window.at[pl.ds(2 * leaves + start, count)], bulk_send, bulk_recv)
        )
    coef_up = onward(0, coefs, cwin.at[pl.ds(0, leaves)], coef_send, coef_recv)
    coef_down = backward(1, coefs, cwin.at[pl.ds(2 * leaves, leaves)], coef_send, coef_recv)

    def start_up(copies):
        @pl.when(has_next)
        def _():
            for copy in copies:
                copy.start()

    def start_down(copies):
        @pl.when(has_prev)
        def _():
            for copy in copies:
                copy.start()

    def finish(up_copies, down_copies):
        @pl.when(has_next)
        def _():
            for copy in up_copies:
                copy.wait_send()
            for copy in down_copies:
                copy.wait_recv()

        @pl.when(has_prev)
        def _():
            for copy in up_copies:
                copy.wait_recv()
            for copy in down_copies:
                copy.wait_send()

    edge = sub == n_sub - 1
    place = lax.rem(col, 2 * side)
    leads = edge & (place == 2 * side - 1)
    yields = edge & (place == 2 * side - 2)

    @pl.when(has_next & jnp.logical_not(yields))
    def _():
        up[0].start()

    @pl.when(has_next & leads)
    def _():
        up[1].start()

    signal(known.at[0], along(1))

    @pl.when(has_next)
    def _():
        signal(known.at[1], following)

    @pl.when(sub == n_sub - 1)
    def _():
        signal(known.at[2], at_sub(1))

    @pl.when(has_prev)
    def _():
        pl.semaphore_wait(known.at[1], 1)

    start_down(down[:1])

    @pl.when(sub == 0)
    def _():
        pl.semaphore_wait(known.at[2], 1)

    def tell(number, targets):
        for target in targets:
            signal(known.at[number], target)

    tell(3, (at_sub(1), at_sub(-1)))

    for load in window_loads + [block_load]:
        load.start()

    own_load.wait()
    basis_load.wait()
    for leaf in range(leaves):
        value = matmul(basis[leaf], own[leaf]).astype(BF)
        coefs[leaf] = value
        cwin[leaves + leaf] = value

    pl.semaphore_wait(known.at[3], 2)
    tell(5, (at_sub(2), at_sub(-2)))
    pl.semaphore_wait(known.at[0], 1)
    tell(4, (along(1), along(-1)))

    for load in transfer_loads:
        load.wait()
    cluster_coef = matmul_t(
        transfer[...].reshape(leaves * rank, rank).astype(BF), coefs[...].reshape(leaves * rank, cols)
    )
    zsend[0:rank] = cluster_coef.astype(BF)
    tall = rank * rank // cols
    zsend[rank : rank + tall] = jnp.concatenate(
        [c_transfer[0, tall * q : tall * (q + 1)] for q in range(rank // tall)], axis=1
    ).astype(BF)

    pl.semaphore_wait(known.at[5], 2)
    z_copies = [
        pltpu.make_async_remote_copy(
            src_ref=zsend,
            dst_ref=zbuf.at[sub],
            send_sem=z_send.at[j],
            recv_sem=z_recv.at[j],
            device_id=at_sub(j),
            device_id_type=MESH,
        )
        for j in range(1, n_sub)
    ]
    for copy in z_copies:
        copy.start()
    @pl.when(has_next & yields)
    def _():
        up[0].start()

    start_up([coef_up])

    @pl.when(has_next & jnp.logical_not(leads))
    def _():
        up[1].start()

    start_up(up[2:])
    start_down([coef_down] + down[1:])
    keep_z = pltpu.make_async_copy(zsend, zbuf.at[sub], load_sem.at[10])
    keep_z.start()
    table_loads = [
        pltpu.make_async_copy(source, target, table_sem.at[i])
        for i, (source, target) in enumerate(
            ((near_table, near_index), (far_table, leaf_far), (cluster_table, cluster_partner), (top_table, top_partner))
        )
    ]
    for load in [coupling_load] + tree_loads + table_loads:
        load.start()
    pl.semaphore_wait(known.at[4], 2)
    tell(6, (along(2), along(-2)))

    block_load.wait()

    def own_product(leaf, carry):
        acc[leaf] = matmul(blocks[leaf, 0], own[leaf])
        packed[leaf] = jnp.concatenate([blocks[leaf, k, :, rows_a:rows] for k in range(1, near)], axis=1)
        return carry

    lax.fori_loop(0, leaves // 2, own_product, 0, unroll=2)
    pl.semaphore_wait(known.at[6], 2)
    tell(7, (along(4), along(-4)))
    lax.fori_loop(leaves // 2, leaves, own_product, 0, unroll=2)
    pl.semaphore_wait(known.at[7], 2)
    tell(8, (along(8), along(-8)))

    keep_z.wait()
    for copy in z_copies:
        copy.wait()
    gathered = zbuf[...].astype(F32)
    top = jnp.zeros((rank, cols), F32)
    for q in range(rank // tall):
        left = gathered[:, rank : rank + tall, rank * q : rank * (q + 1)].reshape(n_sub * tall, rank)
        right = gathered[:, tall * q : tall * (q + 1)].reshape(n_sub * tall, cols)
        top = top + matmul_t(left.astype(BF), right.astype(BF))
    tsend[...] = top.astype(BF)

    def top_copy(j):
        return pltpu.make_async_remote_copy(
            src_ref=tsend,
            dst_ref=tbuf.at[col],
            send_sem=t_send.at[j],
            recv_sem=t_recv.at[j],
            device_id=at_col(j),
            device_id_type=MESH,
        )

    def start_top(j, carry):
        top_copy(j).start()
        return carry

    def wait_top(j, carry):
        top_copy(j).wait()
        return carry

    pl.semaphore_wait(known.at[8], 2)
    lax.fori_loop(1, n_col, start_top, 0)
    keep_t = pltpu.make_async_copy(tsend, tbuf.at[col], load_sem.at[10])
    keep_t.start()

    for load in [coupling_load] + tree_loads + table_loads:
        load.wait()
    cluster_field = jnp.zeros((rank, cols), F32)
    for k in range(c_coupling.shape[1]):
        cluster_field = cluster_field + matmul(c_coupling[0, k].astype(BF), zbuf[cluster_partner[0, k], 0:rank])

    finish([coef_up], [coef_down])

    def far_sum(leaf, carry):
        left = jnp.concatenate([coupling[leaf, k] for k in range(far0)], axis=1).astype(BF)
        right = jnp.concatenate([cwin[within(leaf_far[k, leaf])] for k in range(far0)], axis=0)
        field[leaf] = matmul(left, right)
        return carry

    lax.fori_loop(0, leaves, far_sum, 0, unroll=4)

    keep_t.wait()
    lax.fori_loop(1, n_col, wait_top, 0)
    top_field = jnp.zeros((rank, cols), F32)
    for k in range(t_coupling.shape[1]):
        top_field = top_field + matmul(t_coupling[0, k].astype(BF), tbuf[top_partner[0, k]])
    cluster_field = cluster_field + matmul(c_transfer[0].astype(BF), top_field.astype(BF))
    parent = cluster_field.astype(BF)

    def far_product(leaf, carry):
        value = field[leaf] + matmul(transfer[leaf].astype(BF), parent)
        acc[leaf] += matmul_t(basis[leaf], value.astype(BF))
        return carry

    lax.fori_loop(0, leaves, far_product, 0, unroll=4)

    for load in window_loads:
        load.wait()
    finish(up[:3], down[:3])

    def near_first(leaf, carry):
        value = acc[leaf]
        for k in range(1, near):
            value = value + matmul(blocks[leaf, k, :, 0:rows_a], win_a[within(near_index[k, leaf])])
        acc[leaf] = value
        return carry

    lax.fori_loop(0, leaves, near_first, 0, unroll=4)
    finish(up[3:], down[3:])

    def near_second(leaf, carry):
        right = jnp.concatenate([win_b[within(near_index[k, leaf])] for k in range(1, near)], axis=0)
        out[leaf] = (acc[leaf] + matmul(packed[leaf], right)).astype(BF)
        return carry

    lax.fori_loop(0, leaves, near_second, 0, unroll=True)


def local(n_col, n_sub, *args):
    (
        vectors,
        near_blocks,
        near_index,
        leaf_basis,
        leaf_transfer,
        leaf_coupling,
        leaf_far,
        cluster_transfer,
        cluster_coupling,
        cluster_partner,
        top_coupling,
        top_partner,
    ) = args
    leaves, rank, rows = leaf_basis.shape
    near = near_blocks.shape[1]
    cols = vectors.shape[1]
    rows_b = rows // 4
    rows_a = rows - rows_b
    anywhere = pl.BlockSpec(memory_space=pl.ANY)
    scalars = anywhere
    dma = pltpu.SemaphoreType.DMA
    out = pl.pallas_call(
        functools.partial(kernel, n_col, n_sub, math.isqrt(n_col // 2), 5, 3),
        out_shape=pltpu.VMEM((leaves, rows, cols), BF),
        in_specs=[
            anywhere,
            anywhere,
            scalars,
            anywhere,
            anywhere,
            anywhere,
            scalars,
            anywhere,
            anywhere,
            scalars,
            anywhere,
            scalars,
        ],
        out_specs=pl.BlockSpec(memory_space=pltpu.VMEM),
        scratch_shapes=[
            pltpu.VMEM((leaves, rows, cols), BF),
            pltpu.VMEM((3 * leaves, rows_a, cols), BF),
            pltpu.VMEM((3 * leaves, rows_b, cols), BF),
            pltpu.VMEM(near_blocks.shape, BF),
            pltpu.VMEM((leaves, rows, (near - 1) * rows_b), BF),
            pltpu.VMEM(leaf_basis.shape, BF),
            pltpu.VMEM(leaf_transfer.shape, F32),
            pltpu.VMEM(leaf_coupling.shape, F32),
            pltpu.VMEM(cluster_transfer.shape, F32),
            pltpu.VMEM(cluster_coupling.shape, F32),
            pltpu.VMEM(top_coupling.shape, F32),
            pltpu.VMEM((leaves, rank, cols), BF),
            pltpu.VMEM((3 * leaves, rank, cols), BF),
            pltpu.VMEM((rank + rank * rank // cols, cols), BF),
            pltpu.VMEM((n_sub, rank + rank * rank // cols, cols), BF),
            pltpu.VMEM((rank, cols), BF),
            pltpu.VMEM((n_col, rank, cols), BF),
            pltpu.VMEM((leaves, rank, cols), F32),
            pltpu.VMEM((leaves, rows, cols), F32),
            dma((11,)),
            dma((8,)),
            dma((8,)),
            dma((2,)),
            dma((2,)),
            dma((n_sub,)),
            dma((n_sub,)),
            dma((n_col,)),
            dma((n_col,)),
            pltpu.SemaphoreType.REGULAR((9,)),
            dma((4,)),
            pltpu.SMEM((near, leaves), jnp.int32),
            pltpu.SMEM((leaf_far.shape[1], leaves), jnp.int32),
            pltpu.SMEM(cluster_partner.shape, jnp.int32),
            pltpu.SMEM(top_partner.shape, jnp.int32),
        ],
        compiler_params=pltpu.CompilerParams(collective_id=0, has_side_effects=True),
    )(
        vectors.reshape(leaves, rows, cols),
        near_blocks,
        near_index.T,
        leaf_basis,
        leaf_transfer,
        leaf_coupling,
        leaf_far.T,
        cluster_transfer,
        cluster_coupling,
        cluster_partner,
        top_coupling,
        top_partner,
    )
    return out.reshape(leaves * rows, cols)


def solution(mesh):
    leaf = ("col", "sub")
    in_specs = (
        P(leaf, None),
        P(leaf, None, None, None),
        P(leaf, None),
        P(leaf, None, None),
        P(leaf, None, None),
        P(leaf, None, None, None),
        P(leaf, None),
        P(leaf, None, None),
        P(leaf, None, None, None),
        P(leaf, None),
        P("col", None, None, None),
        P("col", None),
    )
    body = functools.partial(local, mesh.shape["col"], mesh.shape["sub"])
    return jax.shard_map(body, mesh=mesh, in_specs=in_specs, out_specs=P(leaf, None), check_vma=False)
```

```python
import functools
import math

import jax
import jax.numpy as jnp
from jax import lax
from jax.experimental import pallas as pl
from jax.experimental.pallas import tpu as pltpu
from jax.sharding import PartitionSpec as P

MESH = pl.DeviceIdType.MESH
BF = jnp.bfloat16
F32 = jnp.float32


def matmul(a, b):
    return jnp.dot(a, b, preferred_element_type=F32)


def matmul_t(a, b):
    return lax.dot_general(a, b, (((0,), (0,)), ((), ())), preferred_element_type=F32)


def kernel(
    n_col,
    n_sub,
    side,
    first,
    more,
    vec,
    near_blocks,
    near_table,
    leaf_basis,
    leaf_transfer,
    leaf_coupling,
    far_table,
    cluster_transfer,
    cluster_coupling,
    cluster_table,
    top_coupling,
    top_table,
    out,
    own,
    win_a,
    win_b,
    blocks,
    packed,
    basis,
    transfer,
    coupling,
    c_transfer,
    c_coupling,
    t_coupling,
    coefs,
    cwin,
    zsend,
    zbuf,
    tsend,
    tbuf,
    field,
    acc,
    load_sem,
    bulk_send,
    bulk_recv,
    coef_send,
    coef_recv,
    z_send,
    z_recv,
    t_send,
    t_recv,
    known,
    table_sem,
    near_index,
    leaf_far,
    cluster_partner,
    top_partner,
):
    leaves, rows, cols = own.shape
    near = blocks.shape[1]
    far0 = coupling.shape[1]
    rank = basis.shape[1]
    rows_a, rows_b = win_a.shape[1], win_b.shape[1]
    col = lax.axis_index("col")
    sub = lax.axis_index("sub")
    here = col * n_sub + sub
    total = n_col * n_sub
    window_start = (here - 1) * leaves
    has_next = here < total - 1
    has_prev = here > 0

    def within(leaf):
        return jnp.minimum(jnp.maximum(leaf - window_start, 0), 3 * leaves - 1)

    def device(index):
        return (index // n_sub, lax.rem(index, n_sub))

    following = device(lax.rem(here + 1, total))
    previous = device(lax.rem(here + total - 1, total))

    def at_col(step):
        return (lax.rem(col + step + n_col, n_col), sub)

    def walk(position):
        line, place = position // (2 * side), lax.rem(position, 2 * side)
        chip, core = place // 2, lax.rem(place, 2)
        odd = lax.rem(line, 2)
        return line * 2 * side + (odd * (side - 1) + (1 - 2 * odd) * chip) * 2 + core

    def along(step):
        return (walk(lax.rem(walk(col) + step + n_col, n_col)), sub)

    def at_sub(step):
        return (col, lax.rem(sub + step + n_sub, n_sub))

    def signal(sem, target):
        pl.semaphore_signal(sem, inc=1, device_id=target, device_id_type=MESH)

    barrier = pltpu.get_barrier_semaphore()
    signal(barrier, along(1))

    @pl.when(has_prev)
    def _():
        signal(barrier, previous)

    @pl.when(sub == 0)
    def _():
        signal(barrier, at_sub(-1))

    own_load = pltpu.make_async_copy(vec, own, load_sem.at[0])
    basis_load = pltpu.make_async_copy(leaf_basis, basis, load_sem.at[1])
    transfer_loads = [
        pltpu.make_async_copy(leaf_transfer, transfer, load_sem.at[2]),
        pltpu.make_async_copy(cluster_transfer, c_transfer, load_sem.at[3]),
    ]
    block_load = pltpu.make_async_copy(near_blocks, blocks, load_sem.at[4])
    coupling_load = pltpu.make_async_copy(leaf_coupling, coupling, load_sem.at[5])
    window_loads = [
        pltpu.make_async_copy(vec.at[:, pl.ds(0, rows_a)], win_a.at[pl.ds(leaves, leaves)], load_sem.at[6]),
        pltpu.make_async_copy(vec.at[:, pl.ds(rows_a, rows_b)], win_b.at[pl.ds(leaves, leaves)], load_sem.at[7]),
    ]
    tree_loads = [
        pltpu.make_async_copy(cluster_coupling, c_coupling, load_sem.at[8]),
        pltpu.make_async_copy(top_coupling, t_coupling, load_sem.at[9]),
    ]
    for load in [own_load, basis_load] + transfer_loads:
        load.start()

    greeted = 1 + jnp.where(has_next, 1, 0) + jnp.where(sub == n_sub - 1, 1, 0)
    pl.semaphore_wait(barrier, greeted)

    def onward(number, source, window, send_sem, recv_sem):
        return pltpu.make_async_remote_copy(
            src_ref=source,
            dst_ref=window,
            send_sem=send_sem.at[number],
            recv_sem=recv_sem.at[number],
            device_id=following,
            device_id_type=MESH,
        )

    def backward(number, source, window, send_sem, recv_sem):
        return pltpu.make_async_remote_copy(
            src_ref=source,
            dst_ref=window,
            send_sem=send_sem.at[number],
            recv_sem=recv_sem.at[number],
            device_id=previous,
            device_id_type=MESH,
        )

    parts = [
        (win_a, 0, rows_a, 0, first),
        (win_a, 0, rows_a, first, more),
        (win_a, 0, rows_a, first + more, leaves - first - more),
        (win_b, rows_a, rows_b, 0, leaves),
    ]
    up, down = [], []
    for number, (window, row, height, start, count) in enumerate(parts):
        source = vec.at[pl.ds(start, count), pl.ds(row, height)]
        up.append(onward(2 * number, source, window.at[pl.ds(start, count)], bulk_send, bulk_recv))
        down.append(
            backward(2 * number + 1, source, window.at[pl.ds(2 * leaves + start, count)], bulk_send, bulk_recv)
        )
    coef_up = onward(0, coefs, cwin.at[pl.ds(0, leaves)], coef_send, coef_recv)
    coef_down = backward(1, coefs, cwin.at[pl.ds(2 * leaves, leaves)], coef_send, coef_recv)

    def start_up(copies):
        @pl.when(has_next)
        def _():
            for copy in copies:
                copy.start()

    def start_down(copies):
        @pl.when(has_prev)
        def _():
            for copy in copies:
                copy.start()

    def finish(up_copies, down_copies):
        @pl.when(has_next)
        def _():
            for copy in up_copies:
                copy.wait_send()
            for copy in down_copies:
                copy.wait_recv()

        @pl.when(has_prev)
        def _():
            for copy in up_copies:
                copy.wait_recv()
            for copy in down_copies:
                copy.wait_send()

    edge = sub == n_sub - 1
    place = lax.rem(col, 2 * side)
    leads = edge & ((place == 2 * side - 1) | (col == 0))
    yields = edge & (place == 2 * side - 2)

    @pl.when(has_next & jnp.logical_not(yields))
    def _():
        up[0].start()

    @pl.when(has_next & leads)
    def _():
        up[1].start()

    signal(known.at[0], along(-1))

    @pl.when(has_next)
    def _():
        signal(known.at[1], following)

    @pl.when(sub == n_sub - 1)
    def _():
        signal(known.at[2], at_sub(1))

    @pl.when(has_prev)
    def _():
        pl.semaphore_wait(known.at[1], 1)

    start_down(down[:1])

    @pl.when(sub == 0)
    def _():
        pl.semaphore_wait(known.at[2], 1)

    def tell(number, targets):
        for target in targets:
            signal(known.at[number], target)

    tell(3, (at_sub(1), at_sub(-1)))

    for load in window_loads + [block_load]:
        load.start()

    own_load.wait()
    basis_load.wait()
    for leaf in range(leaves):
        value = matmul(basis[leaf], own[leaf]).astype(BF)
        coefs[leaf] = value
        cwin[leaves + leaf] = value

    pl.semaphore_wait(known.at[3], 2)
    tell(5, (at_sub(2), at_sub(-2)))
    pl.semaphore_wait(known.at[0], 1)
    tell(4, (along(1), along(-1)))

    for load in transfer_loads:
        load.wait()
    cluster_coef = matmul_t(
        transfer[...].reshape(leaves * rank, rank).astype(BF), coefs[...].reshape(leaves * rank, cols)
    )
    zsend[0:rank] = cluster_coef.astype(BF)
    tall = rank * rank // cols
    zsend[rank : rank + tall] = jnp.concatenate(
        [c_transfer[0, tall * q : tall * (q + 1)] for q in range(rank // tall)], axis=1
    ).astype(BF)

    @pl.when(has_next & yields)
    def _():
        up[0].start()

    pl.semaphore_wait(known.at[5], 2)
    z_copies = [
        pltpu.make_async_remote_copy(
            src_ref=zsend,
            dst_ref=zbuf.at[sub],
            send_sem=z_send.at[j],
            recv_sem=z_recv.at[j],
            device_id=at_sub(j),
            device_id_type=MESH,
        )
        for j in range(1, n_sub)
    ]
    for copy in z_copies:
        copy.start()
    start_up([coef_up])

    @pl.when(has_next & jnp.logical_not(leads))
    def _():
        up[1].start()

    start_up(up[2:])
    start_down([coef_down] + down[1:])
    keep_z = pltpu.make_async_copy(zsend, zbuf.at[sub], load_sem.at[10])
    keep_z.start()
    table_loads = [
        pltpu.make_async_copy(source, target, table_sem.at[i])
        for i, (source, target) in enumerate(
            ((near_table, near_index), (far_table, leaf_far), (cluster_table, cluster_partner), (top_table, top_partner))
        )
    ]
    for load in [coupling_load] + tree_loads + table_loads:
        load.start()
    pl.semaphore_wait(known.at[4], 2)
    tell(6, (along(2), along(-2)))

    block_load.wait()

    def own_product(leaf, carry):
        acc[leaf] = matmul(blocks[leaf, 0], own[leaf])
        packed[leaf] = jnp.concatenate([blocks[leaf, k, :, rows_a:rows] for k in range(1, near)], axis=1)
        return carry

    lax.fori_loop(0, leaves // 2, own_product, 0, unroll=2)
    pl.semaphore_wait(known.at[6], 2)
    tell(7, (along(4), along(-4)))
    lax.fori_loop(leaves // 2, leaves, own_product, 0, unroll=2)
    pl.semaphore_wait(known.at[7], 2)
    tell(8, (along(8), along(-8)))

    keep_z.wait()
    for copy in z_copies:
        copy.wait()
    gathered = zbuf[...].astype(F32)
    top = jnp.zeros((rank, cols), F32)
    for q in range(rank // tall):
        left = gathered[:, rank : rank + tall, rank * q : rank * (q + 1)].reshape(n_sub * tall, rank)
        right = gathered[:, tall * q : tall * (q + 1)].reshape(n_sub * tall, cols)
        top = top + matmul_t(left.astype(BF), right.astype(BF))
    tsend[...] = top.astype(BF)

    def top_copy(j):
        return pltpu.make_async_remote_copy(
            src_ref=tsend,
            dst_ref=tbuf.at[col],
            send_sem=t_send.at[j],
            recv_sem=t_recv.at[j],
            device_id=at_col(j),
            device_id_type=MESH,
        )

    def start_top(j, carry):
        top_copy(j).start()
        return carry

    def wait_top(j, carry):
        top_copy(j).wait()
        return carry

    pl.semaphore_wait(known.at[8], 2)
    lax.fori_loop(1, n_col, start_top, 0)
    keep_t = pltpu.make_async_copy(tsend, tbuf.at[col], load_sem.at[10])
    keep_t.start()

    for load in [coupling_load] + tree_loads + table_loads:
        load.wait()
    cluster_field = jnp.zeros((rank, cols), F32)
    for k in range(c_coupling.shape[1]):
        cluster_field = cluster_field + matmul(c_coupling[0, k].astype(BF), zbuf[cluster_partner[0, k], 0:rank])

    finish([coef_up], [coef_down])

    def far_sum(leaf, carry):
        left = jnp.concatenate([coupling[leaf, k] for k in range(far0)], axis=1).astype(BF)
        right = jnp.concatenate([cwin[within(leaf_far[k, leaf])] for k in range(far0)], axis=0)
        field[leaf] = matmul(left, right)
        return carry

    lax.fori_loop(0, leaves, far_sum, 0, unroll=4)

    keep_t.wait()
    lax.fori_loop(1, n_col, wait_top, 0)
    top_field = jnp.zeros((rank, cols), F32)
    for k in range(t_coupling.shape[1]):
        top_field = top_field + matmul(t_coupling[0, k].astype(BF), tbuf[top_partner[0, k]])
    cluster_field = cluster_field + matmul(c_transfer[0].astype(BF), top_field.astype(BF))
    parent = cluster_field.astype(BF)

    def far_product(leaf, carry):
        value = field[leaf] + matmul(transfer[leaf].astype(BF), parent)
        acc[leaf] += matmul_t(basis[leaf], value.astype(BF))
        return carry

    lax.fori_loop(0, leaves, far_product, 0, unroll=4)

    for load in window_loads:
        load.wait()
    finish(up[:3], down[:3])

    def near_first(leaf, carry):
        value = acc[leaf]
        for k in range(1, near):
            value = value + matmul(blocks[leaf, k, :, 0:rows_a], win_a[within(near_index[k, leaf])])
        acc[leaf] = value
        return carry

    lax.fori_loop(0, leaves, near_first, 0, unroll=4)
    finish(up[3:], down[3:])

    def near_second(leaf, carry):
        right = jnp.concatenate([win_b[within(near_index[k, leaf])] for k in range(1, near)], axis=0)
        out[leaf] = (acc[leaf] + matmul(packed[leaf], right)).astype(BF)
        return carry

    lax.fori_loop(0, leaves, near_second, 0, unroll=True)


def local(n_col, n_sub, *args):
    (
        vectors,
        near_blocks,
        near_index,
        leaf_basis,
        leaf_transfer,
        leaf_coupling,
        leaf_far,
        cluster_transfer,
        cluster_coupling,
        cluster_partner,
        top_coupling,
        top_partner,
    ) = args
    leaves, rank, rows = leaf_basis.shape
    near = near_blocks.shape[1]
    cols = vectors.shape[1]
    rows_b = rows // 4
    rows_a = rows - rows_b
    anywhere = pl.BlockSpec(memory_space=pl.ANY)
    scalars = anywhere
    dma = pltpu.SemaphoreType.DMA
    out = pl.pallas_call(
        functools.partial(kernel, n_col, n_sub, math.isqrt(n_col // 2), 5, 3),
        out_shape=pltpu.VMEM((leaves, rows, cols), BF),
        in_specs=[
            anywhere,
            anywhere,
            scalars,
            anywhere,
            anywhere,
            anywhere,
            scalars,
            anywhere,
            anywhere,
            scalars,
            anywhere,
            scalars,
        ],
        out_specs=pl.BlockSpec(memory_space=pltpu.VMEM),
        scratch_shapes=[
            pltpu.VMEM((leaves, rows, cols), BF),
            pltpu.VMEM((3 * leaves, rows_a, cols), BF),
            pltpu.VMEM((3 * leaves, rows_b, cols), BF),
            pltpu.VMEM(near_blocks.shape, BF),
            pltpu.VMEM((leaves, rows, (near - 1) * rows_b), BF),
            pltpu.VMEM(leaf_basis.shape, BF),
            pltpu.VMEM(leaf_transfer.shape, F32),
            pltpu.VMEM(leaf_coupling.shape, F32),
            pltpu.VMEM(cluster_transfer.shape, F32),
            pltpu.VMEM(cluster_coupling.shape, F32),
            pltpu.VMEM(top_coupling.shape, F32),
            pltpu.VMEM((leaves, rank, cols), BF),
            pltpu.VMEM((3 * leaves, rank, cols), BF),
            pltpu.VMEM((rank + rank * rank // cols, cols), BF),
            pltpu.VMEM((n_sub, rank + rank * rank // cols, cols), BF),
            pltpu.VMEM((rank, cols), BF),
            pltpu.VMEM((n_col, rank, cols), BF),
            pltpu.VMEM((leaves, rank, cols), F32),
            pltpu.VMEM((leaves, rows, cols), F32),
            dma((11,)),
            dma((8,)),
            dma((8,)),
            dma((2,)),
            dma((2,)),
            dma((n_sub,)),
            dma((n_sub,)),
            dma((n_col,)),
            dma((n_col,)),
            pltpu.SemaphoreType.REGULAR((9,)),
            dma((4,)),
            pltpu.SMEM((near, leaves), jnp.int32),
            pltpu.SMEM((leaf_far.shape[1], leaves), jnp.int32),
            pltpu.SMEM(cluster_partner.shape, jnp.int32),
            pltpu.SMEM(top_partner.shape, jnp.int32),
        ],
        compiler_params=pltpu.CompilerParams(collective_id=0, has_side_effects=True),
    )(
        vectors.reshape(leaves, rows, cols),
        near_blocks,
        near_index.T,
        leaf_basis,
        leaf_transfer,
        leaf_coupling,
        leaf_far.T,
        cluster_transfer,
        cluster_coupling,
        cluster_partner,
        top_coupling,
        top_partner,
    )
    return out.reshape(leaves * rows, cols)


def solution(mesh):
    leaf = ("col", "sub")
    in_specs = (
        P(leaf, None),
        P(leaf, None, None, None),
        P(leaf, None),
        P(leaf, None, None),
        P(leaf, None, None),
        P(leaf, None, None, None),
        P(leaf, None),
        P(leaf, None, None),
        P(leaf, None, None, None),
        P(leaf, None),
        P("col", None, None, None),
        P("col", None),
    )
    body = functools.partial(local, mesh.shape["col"], mesh.shape["sub"])
    return jax.shard_map(body, mesh=mesh, in_specs=in_specs, out_specs=P(leaf, None), check_vma=False)
```

```python
import functools
import math

import jax
import jax.numpy as jnp
from jax import lax
from jax.experimental import pallas as pl
from jax.experimental.pallas import tpu as pltpu
from jax.sharding import PartitionSpec as P

MESH = pl.DeviceIdType.MESH
BF = jnp.bfloat16
F32 = jnp.float32


def matmul(a, b):
    return jnp.dot(a, b, preferred_element_type=F32)


def matmul_t(a, b):
    return lax.dot_general(a, b, (((0,), (0,)), ((), ())), preferred_element_type=F32)


def kernel(
    n_col,
    n_sub,
    side,
    first,
    more,
    vec,
    near_blocks,
    near_table,
    leaf_basis,
    leaf_transfer,
    leaf_coupling,
    far_table,
    cluster_transfer,
    cluster_coupling,
    cluster_table,
    top_coupling,
    top_table,
    out,
    own,
    win_a,
    win_b,
    blocks,
    packed,
    basis,
    transfer,
    coupling,
    c_transfer,
    c_coupling,
    t_coupling,
    coefs,
    cwin,
    zsend,
    zbuf,
    tsend,
    tbuf,
    field,
    acc,
    load_sem,
    bulk_send,
    bulk_recv,
    coef_send,
    coef_recv,
    z_send,
    z_recv,
    t_send,
    t_recv,
    known,
    table_sem,
    near_index,
    leaf_far,
    cluster_partner,
    top_partner,
):
    leaves, rows, cols = own.shape
    near = blocks.shape[1]
    far0 = coupling.shape[1]
    rank = basis.shape[1]
    rows_a, rows_b = win_a.shape[1], win_b.shape[1]
    col = lax.axis_index("col")
    sub = lax.axis_index("sub")
    here = col * n_sub + sub
    total = n_col * n_sub
    window_start = (here - 1) * leaves
    has_next = here < total - 1
    has_prev = here > 0

    def within(leaf):
        return jnp.minimum(jnp.maximum(leaf - window_start, 0), 3 * leaves - 1)

    def device(index):
        return (index // n_sub, lax.rem(index, n_sub))

    following = device(lax.rem(here + 1, total))
    previous = device(lax.rem(here + total - 1, total))

    def at_col(step):
        return (lax.rem(col + step + n_col, n_col), sub)

    def walk(position):
        line, place = position // (2 * side), lax.rem(position, 2 * side)
        chip, core = place // 2, lax.rem(place, 2)
        odd = lax.rem(line, 2)
        return line * 2 * side + (odd * (side - 1) + (1 - 2 * odd) * chip) * 2 + core

    def along(step):
        return (walk(lax.rem(walk(col) + step + n_col, n_col)), sub)

    def at_sub(step):
        return (col, lax.rem(sub + step + n_sub, n_sub))

    def signal(sem, target):
        pl.semaphore_signal(sem, inc=1, device_id=target, device_id_type=MESH)

    barrier = pltpu.get_barrier_semaphore()
    signal(barrier, along(1))

    @pl.when(has_prev)
    def _():
        signal(barrier, previous)

    @pl.when(sub == 0)
    def _():
        signal(barrier, at_sub(-1))

    own_load = pltpu.make_async_copy(vec, own, load_sem.at[0])
    basis_load = pltpu.make_async_copy(leaf_basis, basis, load_sem.at[1])
    transfer_loads = [
        pltpu.make_async_copy(leaf_transfer, transfer, load_sem.at[2]),
        pltpu.make_async_copy(cluster_transfer, c_transfer, load_sem.at[3]),
    ]
    block_load = pltpu.make_async_copy(near_blocks, blocks, load_sem.at[4])
    coupling_load = pltpu.make_async_copy(leaf_coupling, coupling, load_sem.at[5])
    window_loads = [
        pltpu.make_async_copy(vec.at[:, pl.ds(0, rows_a)], win_a.at[pl.ds(leaves, leaves)], load_sem.at[6]),
        pltpu.make_async_copy(vec.at[:, pl.ds(rows_a, rows_b)], win_b.at[pl.ds(leaves, leaves)], load_sem.at[7]),
    ]
    tree_loads = [
        pltpu.make_async_copy(cluster_coupling, c_coupling, load_sem.at[8]),
        pltpu.make_async_copy(top_coupling, t_coupling, load_sem.at[9]),
    ]
    for load in [own_load, basis_load] + transfer_loads:
        load.start()

    greeted = 1 + jnp.where(has_next, 1, 0) + jnp.where(sub == n_sub - 1, 1, 0)
    pl.semaphore_wait(barrier, greeted)

    def onward(number, source, window, send_sem, recv_sem):
        return pltpu.make_async_remote_copy(
            src_ref=source,
            dst_ref=window,
            send_sem=send_sem.at[number],
            recv_sem=recv_sem.at[number],
            device_id=following,
            device_id_type=MESH,
        )

    def backward(number, source, window, send_sem, recv_sem):
        return pltpu.make_async_remote_copy(
            src_ref=source,
            dst_ref=window,
            send_sem=send_sem.at[number],
            recv_sem=recv_sem.at[number],
            device_id=previous,
            device_id_type=MESH,
        )

    parts = [
        (win_a, 0, rows_a, 0, first),
        (win_a, 0, rows_a, first, more),
        (win_a, 0, rows_a, first + more, leaves - first - more),
        (win_b, rows_a, rows_b, 0, leaves),
    ]
    up, down = [], []
    for number, (window, row, height, start, count) in enumerate(parts):
        source = vec.at[pl.ds(start, count), pl.ds(row, height)]
        up.append(onward(2 * number, source, window.at[pl.ds(start, count)], bulk_send, bulk_recv))
        down.append(
            backward(2 * number + 1, source, window.at[pl.ds(2 * leaves + start, count)], bulk_send, bulk_recv)
        )
    coef_up = onward(0, coefs, cwin.at[pl.ds(0, leaves)], coef_send, coef_recv)
    coef_down = backward(1, coefs, cwin.at[pl.ds(2 * leaves, leaves)], coef_send, coef_recv)

    def start_up(copies):
        @pl.when(has_next)
        def _():
            for copy in copies:
                copy.start()

    def start_down(copies):
        @pl.when(has_prev)
        def _():
            for copy in copies:
                copy.start()

    def finish(up_copies, down_copies):
        @pl.when(has_next)
        def _():
            for copy in up_copies:
                copy.wait_send()
            for copy in down_copies:
                copy.wait_recv()

        @pl.when(has_prev)
        def _():
            for copy in up_copies:
                copy.wait_recv()
            for copy in down_copies:
                copy.wait_send()

    edge = sub == n_sub - 1
    place = lax.rem(col, 2 * side)
    leads = edge & ((place == 2 * side - 1) | (col == 0))
    yields = edge & (place == 2 * side - 2)

    @pl.when(has_next & jnp.logical_not(yields))
    def _():
        up[0].start()

    @pl.when(has_next & leads)
    def _():
        up[1].start()

    signal(known.at[0], along(-1))

    @pl.when(has_next)
    def _():
        signal(known.at[1], following)

    @pl.when(sub == n_sub - 1)
    def _():
        signal(known.at[2], at_sub(1))

    @pl.when(has_prev)
    def _():
        pl.semaphore_wait(known.at[1], 1)

    start_down(down[:1])

    @pl.when(sub == 0)
    def _():
        pl.semaphore_wait(known.at[2], 1)

    def tell(number, targets):
        for target in targets:
            signal(known.at[number], target)

    tell(3, (at_sub(1), at_sub(-1)))

    for load in window_loads + [block_load]:
        load.start()

    own_load.wait()
    basis_load.wait()
    for leaf in range(leaves):
        value = matmul(basis[leaf], own[leaf]).astype(BF)
        coefs[leaf] = value
        cwin[leaves + leaf] = value

    pl.semaphore_wait(known.at[3], 2)
    tell(5, (at_sub(2), at_sub(-2)))
    pl.semaphore_wait(known.at[0], 1)
    tell(4, (along(1), along(-1)))

    for load in transfer_loads:
        load.wait()
    cluster_coef = matmul_t(
        transfer[...].reshape(leaves * rank, rank).astype(BF), coefs[...].reshape(leaves * rank, cols)
    )
    zsend[0:rank] = cluster_coef.astype(BF)
    tall = rank * rank // cols
    zsend[rank : rank + tall] = jnp.concatenate(
        [c_transfer[0, tall * q : tall * (q + 1)] for q in range(rank // tall)], axis=1
    ).astype(BF)

    @pl.when(has_next & yields)
    def _():
        up[0].start()

    pl.semaphore_wait(known.at[5], 2)
    z_copies = [
        pltpu.make_async_remote_copy(
            src_ref=zsend,
            dst_ref=zbuf.at[sub],
            send_sem=z_send.at[j],
            recv_sem=z_recv.at[j],
            device_id=at_sub(j),
            device_id_type=MESH,
        )
        for j in sorted(range(1, n_sub), key=lambda j: -min(j, n_sub - j))
    ]
    for copy in z_copies:
        copy.start()
    start_up([coef_up])

    @pl.when(has_next & jnp.logical_not(leads))
    def _():
        up[1].start()

    start_up(up[2:])
    start_down([coef_down] + down[1:])
    keep_z = pltpu.make_async_copy(zsend, zbuf.at[sub], load_sem.at[10])
    keep_z.start()
    table_loads = [
        pltpu.make_async_copy(source, target, table_sem.at[i])
        for i, (source, target) in enumerate(
            ((near_table, near_index), (far_table, leaf_far), (cluster_table, cluster_partner), (top_table, top_partner))
        )
    ]
    for load in [coupling_load] + tree_loads + table_loads:
        load.start()
    pl.semaphore_wait(known.at[4], 2)
    tell(6, (along(2), along(-2)))

    block_load.wait()

    def own_product(leaf, carry):
        acc[leaf] = matmul(blocks[leaf, 0], own[leaf])
        packed[leaf] = jnp.concatenate([blocks[leaf, k, :, rows_a:rows] for k in range(1, near)], axis=1)
        return carry

    lax.fori_loop(0, leaves // 2, own_product, 0, unroll=2)
    pl.semaphore_wait(known.at[6], 2)
    tell(7, (along(4), along(-4)))
    lax.fori_loop(leaves // 2, leaves, own_product, 0, unroll=2)
    pl.semaphore_wait(known.at[7], 2)
    tell(8, (along(8), along(-8)))

    keep_z.wait()
    for copy in z_copies:
        copy.wait()
    gathered = zbuf[...].astype(F32)
    top = jnp.zeros((rank, cols), F32)
    for q in range(rank // tall):
        left = gathered[:, rank : rank + tall, rank * q : rank * (q + 1)].reshape(n_sub * tall, rank)
        right = gathered[:, tall * q : tall * (q + 1)].reshape(n_sub * tall, cols)
        top = top + matmul_t(left.astype(BF), right.astype(BF))
    tsend[...] = top.astype(BF)

    def top_copy(j):
        return pltpu.make_async_remote_copy(
            src_ref=tsend,
            dst_ref=tbuf.at[col],
            send_sem=t_send.at[j],
            recv_sem=t_recv.at[j],
            device_id=at_col(j),
            device_id_type=MESH,
        )

    def start_top(j, carry):
        top_copy(j).start()
        return carry

    def wait_top(j, carry):
        top_copy(j).wait()
        return carry

    pl.semaphore_wait(known.at[8], 2)
    lax.fori_loop(1, n_col, start_top, 0)
    keep_t = pltpu.make_async_copy(tsend, tbuf.at[col], load_sem.at[10])
    keep_t.start()

    for load in [coupling_load] + tree_loads + table_loads:
        load.wait()
    cluster_field = jnp.zeros((rank, cols), F32)
    for k in range(c_coupling.shape[1]):
        cluster_field = cluster_field + matmul(c_coupling[0, k].astype(BF), zbuf[cluster_partner[0, k], 0:rank])

    finish([coef_up], [coef_down])

    def far_sum(leaf, carry):
        left = jnp.concatenate([coupling[leaf, k] for k in range(far0)], axis=1).astype(BF)
        right = jnp.concatenate([cwin[within(leaf_far[k, leaf])] for k in range(far0)], axis=0)
        field[leaf] = matmul(left, right)
        return carry

    lax.fori_loop(0, leaves, far_sum, 0, unroll=4)

    keep_t.wait()
    lax.fori_loop(1, n_col, wait_top, 0)
    top_field = jnp.zeros((rank, cols), F32)
    for k in range(t_coupling.shape[1]):
        top_field = top_field + matmul(t_coupling[0, k].astype(BF), tbuf[top_partner[0, k]])
    cluster_field = cluster_field + matmul(c_transfer[0].astype(BF), top_field.astype(BF))
    parent = cluster_field.astype(BF)

    def far_product(leaf, carry):
        value = field[leaf] + matmul(transfer[leaf].astype(BF), parent)
        acc[leaf] += matmul_t(basis[leaf], value.astype(BF))
        return carry

    lax.fori_loop(0, leaves, far_product, 0, unroll=16)

    for load in window_loads:
        load.wait()
    finish(up[:3], down[:3])

    def near_first(leaf, carry):
        value = acc[leaf]
        for k in range(1, near):
            value = value + matmul(blocks[leaf, k, :, 0:rows_a], win_a[within(near_index[k, leaf])])
        acc[leaf] = value
        return carry

    lax.fori_loop(0, leaves, near_first, 0, unroll=8)
    finish(up[3:], down[3:])

    def near_second(leaf, carry):
        right = jnp.concatenate([win_b[within(near_index[k, leaf])] for k in range(1, near)], axis=0)
        out[leaf] = (acc[leaf] + matmul(packed[leaf], right)).astype(BF)
        return carry

    lax.fori_loop(0, leaves, near_second, 0, unroll=True)


def local(n_col, n_sub, *args):
    (
        vectors,
        near_blocks,
        near_index,
        leaf_basis,
        leaf_transfer,
        leaf_coupling,
        leaf_far,
        cluster_transfer,
        cluster_coupling,
        cluster_partner,
        top_coupling,
        top_partner,
    ) = args
    leaves, rank, rows = leaf_basis.shape
    near = near_blocks.shape[1]
    cols = vectors.shape[1]
    rows_b = rows // 4
    rows_a = rows - rows_b
    anywhere = pl.BlockSpec(memory_space=pl.ANY)
    scalars = anywhere
    dma = pltpu.SemaphoreType.DMA
    out = pl.pallas_call(
        functools.partial(kernel, n_col, n_sub, math.isqrt(n_col // 2), 5, 3),
        out_shape=pltpu.VMEM((leaves, rows, cols), BF),
        in_specs=[
            anywhere,
            anywhere,
            scalars,
            anywhere,
            anywhere,
            anywhere,
            scalars,
            anywhere,
            anywhere,
            scalars,
            anywhere,
            scalars,
        ],
        out_specs=pl.BlockSpec(memory_space=pltpu.VMEM),
        scratch_shapes=[
            pltpu.VMEM((leaves, rows, cols), BF),
            pltpu.VMEM((3 * leaves, rows_a, cols), BF),
            pltpu.VMEM((3 * leaves, rows_b, cols), BF),
            pltpu.VMEM(near_blocks.shape, BF),
            pltpu.VMEM((leaves, rows, (near - 1) * rows_b), BF),
            pltpu.VMEM(leaf_basis.shape, BF),
            pltpu.VMEM(leaf_transfer.shape, F32),
            pltpu.VMEM(leaf_coupling.shape, F32),
            pltpu.VMEM(cluster_transfer.shape, F32),
            pltpu.VMEM(cluster_coupling.shape, F32),
            pltpu.VMEM(top_coupling.shape, F32),
            pltpu.VMEM((leaves, rank, cols), BF),
            pltpu.VMEM((3 * leaves, rank, cols), BF),
            pltpu.VMEM((rank + rank * rank // cols, cols), BF),
            pltpu.VMEM((n_sub, rank + rank * rank // cols, cols), BF),
            pltpu.VMEM((rank, cols), BF),
            pltpu.VMEM((n_col, rank, cols), BF),
            pltpu.VMEM((leaves, rank, cols), F32),
            pltpu.VMEM((leaves, rows, cols), F32),
            dma((11,)),
            dma((8,)),
            dma((8,)),
            dma((2,)),
            dma((2,)),
            dma((n_sub,)),
            dma((n_sub,)),
            dma((n_col,)),
            dma((n_col,)),
            pltpu.SemaphoreType.REGULAR((9,)),
            dma((4,)),
            pltpu.SMEM((near, leaves), jnp.int32),
            pltpu.SMEM((leaf_far.shape[1], leaves), jnp.int32),
            pltpu.SMEM(cluster_partner.shape, jnp.int32),
            pltpu.SMEM(top_partner.shape, jnp.int32),
        ],
        compiler_params=pltpu.CompilerParams(collective_id=0, has_side_effects=True),
    )(
        vectors.reshape(leaves, rows, cols),
        near_blocks,
        near_index.T,
        leaf_basis,
        leaf_transfer,
        leaf_coupling,
        leaf_far.T,
        cluster_transfer,
        cluster_coupling,
        cluster_partner,
        top_coupling,
        top_partner,
    )
    return out.reshape(leaves * rows, cols)


def solution(mesh):
    leaf = ("col", "sub")
    in_specs = (
        P(leaf, None),
        P(leaf, None, None, None),
        P(leaf, None),
        P(leaf, None, None),
        P(leaf, None, None),
        P(leaf, None, None, None),
        P(leaf, None),
        P(leaf, None, None),
        P(leaf, None, None, None),
        P(leaf, None),
        P("col", None, None, None),
        P("col", None),
    )
    body = functools.partial(local, mesh.shape["col"], mesh.shape["sub"])
    return jax.shard_map(body, mesh=mesh, in_specs=in_specs, out_specs=P(leaf, None), check_vma=False)
```
